128 devices in a mesh: shard: 64 (over z, y, x), rep: 2 (over core).
Axes of the slice: x: 4, y: 4, z: 4, core: 2. Of those that a mesh axis runs over, the one named last changes fastest.
Arguments:
- user_emb: bfloat16 [1024, 1024, 256], P('shard', 'rep'), may hold values from -6 to 6
- elig_owner: int32 [1024, 4], P('shard'), may hold values from 0 to 63, all different within a row; in each aligned block of 16 rows (0 to 15, 16 to 31, ...) at most 2 rows name the same one
- elig_local: int32 [1024, 4], P('shard'), may hold values from 0 to 127
- cluster_size: int32 [1024], P('shard'), may hold values from 1 to 1024, 655360 in all
- camp_emb: bfloat16 [8192, 128, 256], P('shard'), may hold values from -6 to 6
- camp_count: int32 [8192], P('shard'), may hold values from 1 to 128, 786432 in all
- dual_init: float32 [8192, 128], P('shard'), may hold values from 0 to 2
- spend_limit: float32 [8192, 128], P('shard'), may hold values from 0.1 to 10
Outputs:
- user_dual: float32 [1024, 1024], P('shard', 'rep')
- campaign_dual: float32 [8192, 128], P('shard')
The draws below stay inside these ranges and needn't reach their ends.
Inputs may be any that keep to these rules, and one draw needn't show every extreme that they name: `elig_owner`: each row names 4 different owners; among the 16 rows of one shard index no owner is named more than 2 times.
All inputs are finite; a program needn't handle non-finite values. No bound on the sum of `cluster_size` or of `camp_count` on one device may be relied on, other than what follows from the above.
Results may differ from the reference program's by a relative error of at most 0.0015.
Values may be sent and summed in bfloat16 or wider, within the bound.
A program may use at most 128 MiB of HBM per device.

```python
import math
import jax
import jax.numpy as jnp
import numpy as np
from jax import lax

H = 256
CB = 128
E = 4
CS = 1024
CL_DEV = 16
BL_DEV = 128
CAP = 2
CLUSTERS = 1024
NBLOCKS = 8192
N_SHARD = 64


def place_ends(array, stream_key, least, top_value):
    index_at = [jax.random.randint(jax.random.fold_in(stream_key, axis), (), 0, length) for axis, length in enumerate(array.shape)]
    longest = array.shape.index(max(array.shape))
    neighbour = index_at[:longest] + [(index_at[longest] + 1) % array.shape[longest]] + index_at[longest + 1:]
    return array.at[tuple(index_at)].set(least).at[tuple(neighbour)].set(top_value)


def block_levels(rng, extent, pieces, least, high):
    loudness, own = 1.0, jax.random.fold_in(rng, 6)
    for position, shards_of in pieces:
        steps = jnp.exp(jax.random.uniform(jax.random.fold_in(own, position), (shards_of,), jnp.float32, least / len(pieces), high / len(pieces)))
        loudness = loudness * jnp.repeat(steps, extent[position] // shards_of).reshape([-1 if axis == position else 1 for axis in range(len(extent))])
    return loudness


def length_profile(number_of, total, reach, lean):
    loads = [(1 << 20) // math.isqrt(standing ** lean) + 1 for standing in range(2, number_of + 1)]
    surplus, given = total - reach - (number_of - 1), [1] * (number_of - 1)
    while surplus > 0:
        movable = [i for i in range(number_of - 1) if given[i] < reach]
        mass, left = sum([loads[i] for i in movable]), surplus
        for i in movable:
            more = min(reach - given[i], max(1, left * loads[i] // mass), surplus)
            given[i] = given[i] + more
            surplus = surplus - more
    return np.array([reach] + given)


def ragged_sizes(key, amount, total, most, lean):
    if amount == 2:
        one = jax.random.randint(key, (), max(1, total - most), min(most, total - 1) + 1)
        return jnp.stack([one, total - one])
    tallies = jnp.asarray(length_profile(amount, total, most, lean), jnp.int32)
    pairs = (amount - 1) // 2
    giver, sink = tallies[1:1 + 2 * pairs:2], tallies[2:2 + 2 * pairs:2]
    margin = jnp.minimum(giver - 1, most - sink)
    shifted = jax.random.randint(jax.random.fold_in(key, 1), (pairs,), 0, 1 << 20) % (margin + 1)
    tallies = tallies.at[1:1 + 2 * pairs:2].set(giver - shifted).at[2:2 + 2 * pairs:2].set(sink + shifted)
    return tallies[jax.random.permutation(jax.random.fold_in(key, 2), amount)]


def deal_out(rng, own, number, rows, number_of, top, reach, slope):
    sequence = jax.random.permutation(rng, number_of)
    crowded, ordinary = portions_of(number_of, rows * top, reach, slope, True), portions_of(number_of, rows * top, reach, slope, False)
    places = jnp.arange(number_of)

    def named(tallies, offset_by):
        used = int((tallies > 0).sum())
        fixed = max(1, used // 4)
        shifted = fixed + (places - fixed + offset_by * (used - fixed)) % max(1, number_of - fixed)
        return jnp.zeros((number_of,), jnp.int32).at[sequence[jnp.where(places < fixed, places, shifted)]].set(jnp.asarray(tallies, jnp.int32))

    tallies = jnp.where(number % 4 == 0, named(crowded, number // 4), named(ordinary, number - number // 4 - 1))
    mixed = jax.random.permutation(jax.random.fold_in(own, 3), number_of)
    donor, sink = mixed[0:number_of // 2 * 2:2], mixed[1:number_of // 2 * 2:2]
    margin = jnp.minimum(tallies[donor] - 1, reach - tallies[sink]) // 2
    margin = jnp.where((donor == sequence[0]) | (sink == sequence[0]) | (tallies[sink] == 0), 0, jnp.maximum(margin, 0))
    shifted = jax.random.randint(jax.random.fold_in(own, 4), (number_of // 2,), 0, 1 << 20) % (margin + 1)
    tallies = tallies.at[donor].add(-shifted).at[sink].add(shifted)
    members = jnp.searchsorted(jnp.cumsum(tallies), jnp.arange(rows * top), side="right").astype(jnp.int32)
    listing = members.reshape(top, rows).T
    listing = listing[jax.random.permutation(jax.random.fold_in(own, 1), rows)]
    offset_by = jax.random.randint(jax.random.fold_in(own, 2), (rows, 1), 0, top)
    return jnp.take_along_axis(listing, (jnp.arange(top)[None, :] + offset_by) % top, axis=1)


def portions_of(amount, total, limit, slope, full):
    portions = [(1 << 20) // math.isqrt(standing ** slope) + 1 for standing in range(1, amount + 1)]
    largest = limit if full else min(limit, max(-(-total // amount), total * portions[0] // sum(portions)))
    least = 1 if total - largest >= amount - 1 else 0
    given, surplus = [largest] + [least] * (amount - 1), total - largest - least * (amount - 1)
    while surplus > 0:
        free = [i for i in range(1, amount) if given[i] < largest] or [i for i in range(1, amount) if given[i] < limit]
        pool, remaining = sum([portions[i] for i in free]), surplus
        for i in free:
            extra = min(limit - given[i], max(1, remaining * portions[i] // pool), surplus)
            given[i] = given[i] + extra
            surplus = surplus - extra
    return np.array(given)


def gaussian(key, dims, spread, most, pieces=(), dtype=jnp.bfloat16):
    factor_of = block_levels(key, dims, pieces, -0.22, 0.18) if pieces else 1.0
    values = jax.random.normal(key, dims, jnp.float32) * spread * factor_of
    return jnp.minimum(jnp.maximum(values, -most), most).astype(dtype)


def setup_inputs(seed: int = 0) -> dict:
    splits = jax.random.split(jax.random.key(seed), 9)
    user_emb = gaussian(splits[0], (CLUSTERS, CS, H), 1.0, 6.0, ((0, 64), (1, 2)))
    elig_owner_keys = jax.random.split(jax.random.fold_in(splits[1], 1), CLUSTERS // CL_DEV)
    elig_owner_turns = jax.random.permutation(jax.random.fold_in(splits[1], 3), CLUSTERS // CL_DEV)
    elig_owner = jax.vmap(lambda own, number: deal_out(jax.random.fold_in(splits[1], 2), own, number, CL_DEV, N_SHARD, E, CAP, 2))(elig_owner_keys, elig_owner_turns).reshape((CLUSTERS, E))
    elig_local = place_ends(jax.random.randint(splits[2], (CLUSTERS, E), 0, BL_DEV), jax.random.fold_in(splits[2], 1), 0, BL_DEV - 1).astype(jnp.int32)
    cluster_size = ragged_sizes(splits[3], CLUSTERS, CLUSTERS * CS * 5 // 8, CS, 1).astype(jnp.int32)
    camp_emb = gaussian(splits[4], (NBLOCKS, CB, H), 1.0, 6.0, ((0, 64),))
    camp_count = ragged_sizes(splits[5], NBLOCKS, NBLOCKS * CB * 3 // 4, CB, 1).astype(jnp.int32)
    dual_init = jnp.clip(2.0 * jax.random.uniform(splits[6], (NBLOCKS, CB), jnp.float32) ** block_levels(splits[6], (NBLOCKS, CB), ((0, 64),), -0.2, 0.2), 0.0, 2.0)
    spend_limit = jnp.clip(jnp.exp(math.log(10.0) - 4.6051702 * jax.random.uniform(splits[7], (NBLOCKS, CB), jnp.float32) ** block_levels(splits[7], (NBLOCKS, CB), ((0, 64),), -0.2, 0.2)), 0.1, 10.0)
    return {"user_emb": user_emb, "elig_owner": elig_owner, "elig_local": elig_local, "cluster_size": cluster_size, "camp_emb": camp_emb, "camp_count": camp_count, "dual_init": dual_init, "spend_limit": spend_limit}


epsilon = 1e-06
temper = 0.25
sharpness = 16.0

def reference(user_emb, elig_owner, elig_local, cluster_size, camp_emb, camp_count, dual_init, spend_limit):
    block_ids = (elig_owner * BL_DEV + elig_local).astype(jnp.int32)
    slot_pos = jnp.arange(CS)
    live_users = slot_pos[None, :] < cluster_size[:, None]
    camp_pos = jnp.arange(CB)

    def run(duals):

        def one_cluster(packed):
            emb_rows, blocks, live_u = packed
            user_f = emb_rows.astype(jnp.float32)
            user_scale = lax.rsqrt(lax.optimization_barrier(jnp.mean(user_f * user_f, axis=-1)) + epsilon)
            camp_f = jnp.take(camp_emb, blocks, axis=0).astype(jnp.float32)
            camp_scale = lax.rsqrt(lax.optimization_barrier(jnp.mean(camp_f * camp_f, axis=-1)) + epsilon)
            raw_dots = jnp.einsum('uh,ech->euc', user_f, camp_f)
            scores = sharpness / H * raw_dots * user_scale[None, :, None] * camp_scale[:, None, :]
            dual_rows = jnp.take(duals, blocks, axis=0)
            counts = jnp.take(camp_count, blocks, axis=0)
            live_c = camp_pos[None, :] < counts[:, None]
            weights = jnp.where(live_c[:, None, :], jnp.exp((scores - dual_rows[:, None, :]) / temper), 0.0)
            denominator = 1.0 + lax.optimization_barrier(jnp.sum(weights, axis=(0, 2)))
            user_val = jnp.where(live_u, temper * jnp.log(denominator), 0.0)
            alloc_share = weights / denominator[None, :, None]
            spend_rows = lax.optimization_barrier(jnp.sum(jnp.where(live_u[None, :, None], alloc_share, 0.0), axis=1))
            return (user_val, spend_rows)
        user_val, spend_rows = lax.map(one_cluster, (user_emb, block_ids, live_users))
        spend_total = jax.ops.segment_sum(spend_rows.reshape(-1, CB), block_ids.reshape(-1), num_segments=NBLOCKS)
        return (user_val, spend_total)

    def update(duals, spend_total):
        return jnp.maximum(0.0, duals + temper * jnp.log((spend_total + spend_limit) / (2.0 * spend_limit)))
    first_val, spend_one = run(dual_init)
    duals_one = update(dual_init, spend_one)
    second_val, spend_two = run(duals_one)
    duals_two = update(duals_one, spend_two)
    user_dual, spend_last = run(duals_two)
    return (user_dual, duals_two)
```

```python
import functools
import math

import jax
import jax.numpy as jnp
from jax import lax
from jax.experimental import pallas as pl
from jax.experimental.pallas import tpu as pltpu
from jax.sharding import PartitionSpec as P

epsilon = 1e-06
temper = 0.25
sharpness = 16.0
HIGH = lax.Precision.HIGHEST
MESH = pl.DeviceIdType.MESH


def shift_digits(a, b, radix, sign):
    out = 0
    for place in (1, radix, radix * radix):
        digit = ((a // place) % radix + sign * ((b // place) % radix) + radix) % radix
        out = out + digit * place
    return out


def kernel(
    radix,
    item_slot,
    wanted,
    sizes,
    counts,
    dual_init,
    limits,
    to_slots,
    to_items,
    camp_hbm,
    user_hbm,
    user_out,
    dual_out,
    camps,
    users,
    user_scale,
    sendbuf,
    recvbuf,
    kmat,
    ids_in,
    ids_smem,
    row_send,
    row_recv,
    den_send,
    den_recv,
    dual_send,
    dual_recv,
    hit,
    hit_t,
    lam,
    vdup,
    camp_sem,
    user_sem,
    smem_sem,
    user_ssem,
    user_rsem,
    ids_ssem,
    ids_rsem,
    bulk_ssem,
    bulk_rsem,
    row_ssem,
    row_rsem,
    den_ssem,
    den_rsem,
    dual_ssem,
    dual_rsem,
):
    me = lax.axis_index("shard")
    rep = lax.axis_index("rep")
    n = wanted.shape[0]
    clusters, half_users, width = user_hbm.shape
    all_users = 2 * half_users
    half = camps.shape[1]
    lanes = 2 * half
    blocks = camps.shape[0]

    my_rows = pl.ds(pl.multiple_of(rep * half, half), half)
    my_users = pl.ds(pl.multiple_of(rep * half_users, half_users), half_users)
    load_camps = pltpu.make_async_copy(camp_hbm.at[:, my_rows, :], camps, camp_sem)
    load_camps.start()
    load_users = pltpu.make_async_copy(user_hbm, users.at[:, my_users, :], user_sem)
    load_users.start()

    barrier = pltpu.get_barrier_semaphore()

    @pl.loop(1, n)
    def _(d):
        pl.semaphore_signal(
            barrier, inc=1, device_id=(shift_digits(me, d, radix, 1), rep), device_id_type=MESH
        )

    pl.semaphore_signal(barrier, inc=1, device_id=(me, 1 - rep), device_id_type=MESH)
    pl.semaphore_wait(barrier, n)

    def remote(src, dst, ssem, rsem, target):
        return pltpu.make_async_remote_copy(
            src_ref=src, dst_ref=dst, send_sem=ssem, recv_sem=rsem,
            device_id=target, device_id_type=MESH,
        )

    def scatter(src, dst, ssem, rsem, sign):
        @pl.loop(1, n)
        def _(d):
            remote(
                src.at[d], dst.at[d], ssem, rsem, (shift_digits(me, d, radix, sign), rep)
            ).start()

    def all_of(src, dst, ssem, rsem):
        rest = pl.ds(1, n - 1)
        return remote(src.at[rest], dst.at[rest], ssem, rsem, (me, 1 - rep))

    scatter(wanted, ids_in, ids_ssem, ids_rsem, -1)
    swap_users = remote(
        user_hbm, users.at[:, my_users, :], user_ssem, user_rsem, (me, 1 - rep)
    )
    swap_users.start()
    ids_in[0] = wanted[0]

    lane = lax.broadcasted_iota(jnp.int32, (1, lanes), 1)
    left = lane < half

    def spread(x):
        rolled = pltpu.roll(x, half, 1)
        mine = left == (rep == 0)
        return jnp.where(mine, x, rolled)

    lam[...] = spread(dual_init[...])
    limit = spread(limits[...])
    live_camps = (lane % half) + rep * half < counts[...]

    def weights_of(duals):
        return jnp.where(live_camps, jnp.exp(duals * (-1.0 / temper)), 0.0)

    vdup[...] = weights_of(lam[...])

    all_of(wanted, ids_in, ids_ssem, ids_rsem).wait()
    to_smem = pltpu.make_async_copy(ids_in, ids_smem, smem_sem)
    to_smem.start()
    ids = ids_in[:, 0, :]
    block_ids = lax.broadcasted_iota(jnp.int32, (n, blocks), 1)
    hit[:n] = (jnp.broadcast_to(ids[:, 0:1], (n, blocks)) == block_ids).astype(jnp.float32)
    hit[n:] = (jnp.broadcast_to(ids[:, 1:2], (n, blocks)) == block_ids).astype(jnp.float32)

    def send_weights(step):
        picked = jnp.dot(hit[...], vdup[...], precision=HIGH, preferred_element_type=jnp.float32)
        row_send[step, :, 0, :] = jnp.where(left, picked[:n], picked[n:])
        scatter(row_send.at[step], row_recv.at[step], row_ssem.at[step], row_rsem.at[step], 1)
        row_recv[step, 0] = row_send[step, 0]

    def wait_rows(step):
        all_of(
            row_send.at[step], row_recv.at[step], row_ssem.at[step], row_rsem.at[step]
        ).wait()
        return row_recv[step, :, 0, :]

    send_weights(0)
    to_smem.wait()
    load_camps.wait()

    @pl.loop(1, n)
    def _(d):
        for j in range(2):
            sendbuf[2 * d + j] = camps[ids_smem[d, 0, j]]
        pair = pl.ds(2 * d, 2)
        remote(
            sendbuf.at[pair], recvbuf.at[pair], bulk_ssem, bulk_rsem,
            (shift_digits(me, d, radix, 1), rep),
        ).start()

    for j in range(2):
        recvbuf[j] = camps[ids_smem[0, 0, j]]

    hit_t[...] = hit[...].T
    load_users.wait()
    swap_users.wait()

    chunk = 256 if all_users % 256 == 0 else all_users
    chunks = all_users // chunk

    @pl.loop(0, clusters * chunks)
    def _(i):
        k = i // chunks
        at = pl.ds(pl.multiple_of((i % chunks) * chunk, chunk), chunk)
        x = users[k, at, :].astype(jnp.float32)
        mean = jnp.sum(x * x, axis=1, keepdims=True) * (1.0 / width)
        user_scale[k, at, :] = jnp.broadcast_to(lax.rsqrt(mean + epsilon), (chunk, 128))

    rest = pl.ds(2, 2 * n - 2)
    remote(sendbuf.at[rest], recvbuf.at[rest], bulk_ssem, bulk_rsem, (me, 1 - rep)).wait()

    factor = sharpness / width / temper * math.log2(math.e)
    fan = item_slot.shape[0] // clusters
    cols = fan * half

    @pl.loop(0, clusters)
    def _(k):
        emb = jnp.concatenate([recvbuf[item_slot[k * fan + e]] for e in range(fan)], axis=0)
        wide = emb.astype(jnp.float32)
        square = wide * wide
        upper = square.astype(jnp.bfloat16)
        lower = (square - upper.astype(jnp.float32)).astype(jnp.bfloat16)
        ones = jnp.ones((16, width), jnp.bfloat16)
        dims = (((1,), (1,)), ((), ()))
        total = lax.dot_general(ones, upper, dims, preferred_element_type=jnp.float32)
        total = total + lax.dot_general(ones, lower, dims, preferred_element_type=jnp.float32)
        camp_scale = lax.rsqrt(total[0:1] * (1.0 / width) + epsilon) * factor
        for c in range(chunks):
            at = pl.ds(c * chunk, chunk)
            raw = lax.dot_general(users[k, at, :], emb, dims, preferred_element_type=jnp.float32)
            scale = user_scale[k, at, :]
            wide_scale = jnp.concatenate([scale] * (cols // 128), axis=1)
            kmat[k, at, :] = jnp.exp2(raw * wide_scale * camp_scale).astype(jnp.bfloat16)

    def split(x):
        upper = x.astype(jnp.bfloat16)
        lower = (x - upper.astype(jnp.float32)).astype(jnp.bfloat16)
        return jnp.concatenate([upper, lower], axis=0)

    row_id = lax.broadcasted_iota(jnp.int32, (clusters, 1), 0)

    def denominator(step, rows):
        rolled = pltpu.roll(rows, half, 1)
        zero = jnp.zeros_like(rows)
        stack = jnp.concatenate(
            [jnp.where(left, rows, zero), jnp.where(left, rolled, zero),
             jnp.where(left, zero, rows), jnp.where(left, zero, rolled)], axis=0)
        table = jnp.dot(to_items[...], stack, precision=HIGH, preferred_element_type=jnp.float32)
        v = split(jnp.concatenate(
            [table[p * clusters:(p + 1) * clusters] for p in range(fan // 2)], axis=1))

        def add(k, acc):
            out = lax.dot_general(
                v, kmat[k], (((1,), (1,)), ((), ())), preferred_element_type=jnp.float32)
            return acc + jnp.where(row_id == k, out[:clusters] + out[clusters:], 0.0)

        part = lax.fori_loop(0, clusters, add, jnp.zeros((clusters, all_users), jnp.float32))
        den_send[step] = part
        swap = remote(
            den_send.at[step], den_recv.at[step], den_ssem.at[step], den_rsem.at[step],
            (me, 1 - rep))
        swap.start()
        swap.wait()
        return 1.0 + (part + den_recv[step])

    live_users = lax.broadcasted_iota(jnp.int32, (clusters, all_users), 1) < sizes[...]

    def sweep(step, rows):
        den = denominator(step, rows)
        q = split(jnp.where(live_users, 1.0 / den, 0.0))

        def add(k, acc):
            out = jnp.dot(q, kmat[k], preferred_element_type=jnp.float32)
            return acc + jnp.where(row_id == k, out[:clusters] + out[clusters:], 0.0)

        sums = lax.fori_loop(0, clusters, add, jnp.zeros((clusters, cols), jnp.float32))
        table = jnp.concatenate(
            [sums[:, p * lanes:(p + 1) * lanes] for p in range(fan // 2)], axis=0)
        rolled = pltpu.roll(table, half, 1)
        zero = jnp.zeros_like(table)
        stack = jnp.concatenate(
            [jnp.where(left, table, zero), jnp.where(left, rolled, zero),
             jnp.where(left, zero, table), jnp.where(left, zero, rolled)], axis=0)
        out = jnp.dot(to_slots[...], stack, precision=HIGH, preferred_element_type=jnp.float32)
        at = 2 * step + 1
        row_send[at, :, 0, :] = out
        scatter(row_send.at[at], row_recv.at[at], row_ssem.at[at], row_rsem.at[at], -1)
        row_recv[at, 0] = row_send[at, 0]
        got = wait_rows(at)
        turned = pltpu.roll(got, half, 1)
        both = jnp.concatenate(
            [jnp.where(left, got, turned), jnp.where(left, turned, got)], axis=0)
        spend = vdup[...] * jnp.dot(
            hit_t[...], both, precision=HIGH, preferred_element_type=jnp.float32)
        duals = jnp.maximum(
            0.0, lam[...] + temper * jnp.log((spend + limit) / (2.0 * limit)))
        lam[...] = duals
        vdup[...] = weights_of(duals)
        send_weights(at + 1)

    sweep(0, wait_rows(0))
    sweep(1, wait_rows(2))
    dual_send[...] = lam[...]
    swap_duals = remote(dual_send, dual_recv, dual_ssem, dual_rsem, (me, 1 - rep))
    swap_duals.start()
    den = denominator(2, wait_rows(4))
    result = jnp.where(live_users, temper * jnp.log(den), 0.0)
    user_out[...] = jnp.where(rep == 0, result[:, :half_users], result[:, half_users:])
    swap_duals.wait()
    dual_out[...] = jnp.where(left == (rep == 0), dual_send[...], dual_recv[...])


def body(
    user_emb, elig_owner, elig_local, cluster_size, camp_emb, camp_count, dual_init, spend_limit
):
    n = lax.axis_size("shard")
    radix = round(n ** (1 / 3))
    clusters, user_slots, width = user_emb.shape
    blocks, block_camps, _ = camp_emb.shape
    fan = elig_owner.shape[1]
    half = block_camps // 2
    me = lax.axis_index("shard")

    owners = elig_owner.reshape(-1)
    local_ids = elig_local.reshape(-1)
    items = owners.shape[0]
    earlier = jnp.arange(items)[None, :] < jnp.arange(items)[:, None]
    rank = jnp.sum(((owners[:, None] == owners[None, :]) & earlier).astype(jnp.int32), axis=1)
    dist = shift_digits(me, owners, radix, -1)
    item_slot = dist * 2 + rank

    slot_ids = jnp.arange(2 * n, dtype=jnp.int32)
    one_hot = item_slot[:, None] == slot_ids[None, :]
    wanted = jnp.sum(jnp.where(one_hot, local_ids[:, None], 0), axis=0).reshape(n, 2)
    first = jnp.arange(128)[None, None, :] == 0
    wanted = jnp.where(first, wanted[:, 0][:, None, None], wanted[:, 1][:, None, None])

    order = one_hot.astype(jnp.float32).reshape(clusters, fan // 2, 2, n, 2)
    order = order.transpose(1, 0, 2, 3, 4).reshape(clusters * fan // 2, 2, n, 2)
    even0, odd0 = order[:, 0, :, 0], order[:, 1, :, 0]
    even1, odd1 = order[:, 0, :, 1], order[:, 1, :, 1]
    to_slots = jnp.concatenate([even0, odd0, odd1, even1], axis=0).T
    to_items = jnp.concatenate([even0, even1, odd1, odd0], axis=1)

    vmem = pl.BlockSpec(memory_space=pltpu.VMEM)
    smem = pl.BlockSpec(memory_space=pltpu.SMEM)
    hbm = pl.BlockSpec(memory_space=pl.ANY)
    bf, f32, i32 = jnp.bfloat16, jnp.float32, jnp.int32
    dma = pltpu.SemaphoreType.DMA
    all_users = 2 * user_slots
    return pl.pallas_call(
        functools.partial(kernel, radix),
        out_shape=(
            jax.ShapeDtypeStruct((clusters, user_slots), f32),
            jax.ShapeDtypeStruct((blocks, block_camps), f32),
        ),
        in_specs=[smem] + [vmem] * 7 + [hbm] * 2,
        out_specs=(vmem, vmem),
        scratch_shapes=[
            pltpu.VMEM((blocks, half, width), bf),
            pltpu.VMEM((clusters, all_users, width), bf),
            pltpu.VMEM((clusters, all_users, 128), f32),
            pltpu.VMEM((2 * n, half, width), bf),
            pltpu.VMEM((2 * n, half, width), bf),
            pltpu.VMEM((clusters, all_users, fan * half), bf),
            pltpu.VMEM((n, 1, 128), i32),
            pltpu.SMEM((n, 1, 128), i32),
            pltpu.VMEM((5, n, 1, block_camps), f32),
            pltpu.VMEM((5, n, 1, block_camps), f32),
            pltpu.VMEM((3, clusters, all_users), f32),
            pltpu.VMEM((3, clusters, all_users), f32),
            pltpu.VMEM((blocks, block_camps), f32),
            pltpu.VMEM((blocks, block_camps), f32),
            pltpu.VMEM((2 * n, blocks), f32),
            pltpu.VMEM((blocks, 2 * n), f32),
            pltpu.VMEM((blocks, block_camps), f32),
            pltpu.VMEM((blocks, block_camps), f32),
            dma, dma, dma, dma, dma, dma, dma, dma, dma,
            dma((5,)), dma((5,)), dma((3,)), dma((3,)), dma, dma,
        ],
        compiler_params=pltpu.CompilerParams(
            collective_id=0, has_side_effects=True, vmem_limit_bytes=56 << 20
        ),
        name="allocate",
    )(
        item_slot, wanted, cluster_size.reshape(clusters, 1), camp_count.reshape(blocks, 1),
        dual_init, spend_limit, to_slots, to_items, camp_emb, user_emb,
    )


def solution(mesh):
    return jax.shard_map(
        body,
        mesh=mesh,
        in_specs=(
            P("shard", "rep", None),
            P("shard", None),
            P("shard", None),
            P("shard"),
            P("shard", None, None),
            P("shard"),
            P("shard", None),
            P("shard", None),
        ),
        out_specs=(P("shard", "rep"), P("shard", None)),
        check_vma=False,
    )
```

```python
import functools
import math

import jax
import jax.numpy as jnp
from jax import lax
from jax.experimental import pallas as pl
from jax.experimental.pallas import tpu as pltpu
from jax.sharding import PartitionSpec as P

epsilon = 1e-06
temper = 0.25
sharpness = 16.0
mix = 37
MESH = pl.DeviceIdType.MESH


def kernel(
    radix,
    owner_ref,
    local_ref,
    size_ref,
    count_ref,
    dual_init,
    limits,
    camp_hbm,
    user_hbm,
    user_out,
    dual_out,
    camps,
    users,
    user_scale,
    sendbuf,
    recvbuf,
    kmat,
    rows_pad,
    wanted,
    slots,
    slots_smem,
    ids_in,
    ids_smem,
    to_slots,
    to_items,
    row_send,
    row_recv,
    den_send,
    den_recv,
    dual_send,
    dual_recv,
    hit,
    hit_t,
    lam,
    vdup,
    camp_sem,
    user_sem,
    smem_sem,
    slot_sem,
    user_ssem,
    user_rsem,
    ids_ssem,
    ids_rsem,
    bulk_ssem,
    bulk_rsem,
    row_ssem,
    row_rsem,
    den_ssem,
    den_rsem,
    dual_ssem,
    dual_rsem,
):
    me = lax.axis_index("shard")
    rep = lax.axis_index("rep")
    n = wanted.shape[0]
    clusters, half_users, width = user_hbm.shape
    all_users = 2 * half_users
    half = camps.shape[1]
    lanes = 2 * half
    blocks = camps.shape[0]

    my_rows = pl.ds(pl.multiple_of(rep * half, half), half)
    my_users = pl.ds(pl.multiple_of(rep * half_users, half_users), half_users)
    load_camps = pltpu.make_async_copy(camp_hbm.at[:, my_rows, :], camps, camp_sem)
    load_camps.start()
    load_users = pltpu.make_async_copy(user_hbm, users.at[:, my_users, :], user_sem)
    load_users.start()

    places = (radix * radix, radix, 1)
    digits = [(me // p) % radix for p in places]
    moved = {
        sign: [
            [((digit + sign * j + radix) % radix) * p for j in range(radix)]
            for digit, p in zip(digits, places)
        ]
        for sign in (1, -1)
    }

    def partner(d, sign):
        return sum(moved[sign][i][(d // p) % radix] for i, p in enumerate(places))

    order = [(i * mix) % n for i in range(1, n)]

    barrier = pltpu.get_barrier_semaphore()
    for d in order:
        pl.semaphore_signal(
            barrier, inc=1, device_id=(partner(d, 1), rep), device_id_type=MESH
        )
    pl.semaphore_signal(barrier, inc=1, device_id=(me, 1 - rep), device_id_type=MESH)

    def remote(src, dst, ssem, rsem, target):
        return pltpu.make_async_remote_copy(
            src_ref=src, dst_ref=dst, send_sem=ssem, recv_sem=rsem,
            device_id=target, device_id_type=MESH,
        )

    def scatter(src, dst, ssem, rsem, sign):
        for d in order:
            remote(src.at[d], dst.at[d], ssem, rsem, (partner(d, sign), rep)).start()

    def all_of(src, dst, ssem, rsem):
        rest = pl.ds(1, n - 1)
        return remote(src.at[rest], dst.at[rest], ssem, rsem, (me, 1 - rep))

    fan, _ = owner_ref.shape
    i32, f32, bf16 = jnp.int32, jnp.float32, jnp.bfloat16
    lane = lax.broadcasted_iota(i32, (1, lanes), 1)
    left = lane < half
    evens, odds = list(range(0, fan, 2)), list(range(1, fan, 2))
    columns = evens + odds + odds + evens

    def column_row(ref):
        rows_pad[...] = jnp.zeros_like(rows_pad)
        rows_pad[0:fan, 0:clusters] = ref[...]
        row = rows_pad[...]
        out = jnp.zeros((1, lanes), i32)
        for at, e in enumerate(columns):
            piece = row[e:e + 1]
            out = out + (pltpu.roll(piece, at * clusters, 1) if at else piece)
        return out

    owner = column_row(owner_ref)
    local = column_row(local_ref)
    dist = jnp.zeros_like(owner)
    shift = radix.bit_length() - 1
    for i, p in enumerate(places):
        digit = lax.shift_right_logical(owner, i32(p.bit_length() - 1)) & (radix - 1)
        dist = dist + ((digits[i] - digit + radix) & (radix - 1)) * p
    mask = dist == lax.broadcasted_iota(i32, (n, lanes), 0)
    from_col = lax.broadcasted_iota(i32, (lanes, lanes), 0)
    to_col = lax.broadcasted_iota(i32, (lanes, lanes), 1)
    cluster_of = clusters - 1
    ahead = (from_col < half) & ((from_col & cluster_of) < (to_col & cluster_of))
    prefix = jnp.dot(
        mask.astype(f32).astype(bf16), ahead.astype(f32).astype(bf16),
        preferred_element_type=f32)
    rank = (lane >= half).astype(i32)
    chosen = mask & (prefix == rank.astype(f32))
    to_slots[...] = chosen.astype(f32).astype(bf16)
    to_items[...] = chosen.astype(f32).T.astype(bf16)
    first = jnp.sum(jnp.where(chosen & left, local, 0), axis=1, keepdims=True)
    second = jnp.sum(jnp.where(chosen & ~left, local, 0), axis=1, keepdims=True)
    wanted[:, 0, :] = jnp.where(lane == 0, first, second)
    slot = lax.broadcasted_iota(i32, (n, lanes), 0) * 2 + rank
    slots[...] = jnp.sum(jnp.where(chosen, slot, 0), axis=0, keepdims=True)
    slots_to_smem = pltpu.make_async_copy(slots, slots_smem, slot_sem)
    slots_to_smem.start()

    pl.semaphore_wait(barrier, n)

    scatter(wanted, ids_in, ids_ssem, ids_rsem, -1)
    swap_users = remote(
        user_hbm, users.at[:, my_users, :], user_ssem, user_rsem, (me, 1 - rep)
    )
    swap_users.start()
    ids_in[0] = wanted[0]

    def spread(x):
        rolled = pltpu.roll(x, half, 1)
        mine = left == (rep == 0)
        return jnp.where(mine, x, rolled)

    lam[...] = spread(dual_init[...])
    limit = spread(limits[...])
    diagonal = from_col == to_col

    def column(row):
        return jnp.sum(jnp.where(diagonal[:blocks], row.astype(f32), 0.0), axis=1, keepdims=True)

    counts = column(count_ref[...])
    camp_pos = jnp.where(left, lane, lane - half) + rep * half
    live_camps = camp_pos.astype(f32) < counts

    def weights_of(duals):
        return jnp.where(live_camps, jnp.exp(duals * (-1.0 / temper)), 0.0)

    vdup[...] = weights_of(lam[...])

    all_of(wanted, ids_in, ids_ssem, ids_rsem).wait()
    to_smem = pltpu.make_async_copy(ids_in, ids_smem, smem_sem)
    to_smem.start()
    ids = ids_in[:, 0, :]
    block_ids = lax.broadcasted_iota(jnp.int32, (n, blocks), 1)
    hits = jnp.concatenate(
        [(jnp.broadcast_to(ids[:, j:j + 1], (n, blocks)) == block_ids).astype(f32)
         for j in range(2)], axis=0)
    hit[...] = hits.astype(bf16)
    hit_t[...] = hits.T.astype(bf16)

    def pick(table, x):
        upper = x.astype(bf16)
        lower = (x - upper.astype(f32)).astype(bf16)
        out = jnp.dot(
            table, jnp.concatenate([upper, lower], axis=1), preferred_element_type=f32)
        return out[:, :lanes] + out[:, lanes:]

    def send_weights(step):
        picked = pick(hit[...], vdup[...])
        row_send[step, :, 0, :] = jnp.where(left, picked[:n], picked[n:])
        scatter(row_send.at[step], row_recv.at[step], row_ssem.at[step], row_rsem.at[step], 1)
        row_recv[step, 0] = row_send[step, 0]

    def wait_rows(step):
        all_of(
            row_send.at[step], row_recv.at[step], row_ssem.at[step], row_rsem.at[step]
        ).wait()
        return row_recv[step, :, 0, :]

    to_smem.wait()
    load_camps.wait()

    def clamp(i, size):
        return jnp.minimum(jnp.maximum(i, 0), size - 1)

    for d in order:
        for j in range(2):
            sendbuf[2 * d + j] = camps[clamp(ids_smem[d, 0, j], blocks)]
        pair = pl.ds(2 * d, 2)
        remote(
            sendbuf.at[pair], recvbuf.at[pair], bulk_ssem, bulk_rsem, (partner(d, 1), rep)
        ).start()

    for j in range(2):
        recvbuf[j] = camps[clamp(ids_smem[0, 0, j], blocks)]

    send_weights(0)
    load_users.wait()
    swap_users.wait()

    chunk = 256 if all_users % 256 == 0 else all_users
    chunks = all_users // chunk

    @pl.loop(0, clusters * chunks)
    def _(i):
        k = i // chunks
        at = pl.ds(pl.multiple_of((i % chunks) * chunk, chunk), chunk)
        x = users[k, at, :].astype(jnp.float32)
        mean = jnp.sum(x * x, axis=1, keepdims=True) * (1.0 / width)
        user_scale[k, at, :] = jnp.broadcast_to(lax.rsqrt(mean + epsilon), (chunk, 128))

    rest = pl.ds(2, 2 * n - 2)
    remote(sendbuf.at[rest], recvbuf.at[rest], bulk_ssem, bulk_rsem, (me, 1 - rep)).wait()

    factor = sharpness / width / temper * math.log2(math.e)
    cols = fan * half

    slots_to_smem.wait()
    first_at = [columns.index(e) * clusters for e in range(fan)]
    second_at = [(columns.index(e, fan)) * clusters for e in range(fan)]

    @pl.loop(0, clusters)
    def _(k):
        emb = jnp.concatenate(
            [recvbuf[clamp(
                slots_smem[0, first_at[e] + k] + slots_smem[0, second_at[e] + k], 2 * n)]
             for e in range(fan)], axis=0)
        wide = emb.astype(jnp.float32)
        square = wide * wide
        upper = square.astype(jnp.bfloat16)
        lower = (square - upper.astype(jnp.float32)).astype(jnp.bfloat16)
        ones = jnp.ones((16, width), jnp.bfloat16)
        dims = (((1,), (1,)), ((), ()))
        total = lax.dot_general(ones, upper, dims, preferred_element_type=jnp.float32)
        total = total + lax.dot_general(ones, lower, dims, preferred_element_type=jnp.float32)
        camp_scale = lax.rsqrt(total[0:1] * (1.0 / width) + epsilon) * factor
        for c in range(chunks):
            at = pl.ds(c * chunk, chunk)
            raw = lax.dot_general(users[k, at, :], emb, dims, preferred_element_type=jnp.float32)
            scale = user_scale[k, at, :]
            wide_scale = jnp.concatenate([scale] * (cols // 128), axis=1)
            kmat[k, at, :] = jnp.exp2(raw * wide_scale * camp_scale).astype(jnp.bfloat16)

    def split(x):
        upper = x.astype(jnp.bfloat16)
        lower = (x - upper.astype(jnp.float32)).astype(jnp.bfloat16)
        return jnp.concatenate([upper, lower], axis=0)

    row_id = lax.broadcasted_iota(jnp.int32, (clusters, 1), 0)

    part = fan * clusters // 2

    def denominator(step, rows):
        picked = pick(to_items[...], rows)
        a, b, c, d = [picked[p * part:(p + 1) * part] for p in range(4)]
        table = jnp.where(left, a + pltpu.roll(d, half, 1), c + pltpu.roll(b, half, 1))
        v = split(jnp.concatenate(
            [table[p * clusters:(p + 1) * clusters] for p in range(fan // 2)], axis=1))

        def add(k, acc):
            out = lax.dot_general(
                v, kmat[k], (((1,), (1,)), ((), ())), preferred_element_type=jnp.float32)
            return acc + jnp.where(row_id == k, out[:clusters] + out[clusters:], 0.0)

        own = lax.fori_loop(0, clusters, add, jnp.zeros((clusters, all_users), f32))
        den_send[step] = own
        swap = remote(
            den_send.at[step], den_recv.at[step], den_ssem.at[step], den_rsem.at[step],
            (me, 1 - rep))
        swap.start()
        swap.wait()
        return 1.0 + (own + den_recv[step])

    sizes = jnp.sum(
        jnp.where(diagonal[:clusters, :clusters], size_ref[...].astype(f32), 0.0),
        axis=1, keepdims=True).astype(i32)
    live_users = lax.broadcasted_iota(i32, (clusters, all_users), 1) < sizes

    def sweep(step, rows):
        den = denominator(step, rows)
        q = split(jnp.where(live_users, 1.0 / den, 0.0))

        def add(k, acc):
            out = jnp.dot(q, kmat[k], preferred_element_type=jnp.float32)
            return acc + jnp.where(row_id == k, out[:clusters] + out[clusters:], 0.0)

        sums = lax.fori_loop(0, clusters, add, jnp.zeros((clusters, cols), jnp.float32))
        table = jnp.concatenate(
            [sums[:, p * lanes:(p + 1) * lanes] for p in range(fan // 2)], axis=0)
        rolled = pltpu.roll(table, half, 1)
        zero = jnp.zeros_like(table)
        stack = jnp.concatenate(
            [jnp.where(left, table, zero), jnp.where(left, rolled, zero),
             jnp.where(left, zero, table), jnp.where(left, zero, rolled)], axis=0)
        out = pick(to_slots[...], stack)
        at = 2 * step + 1
        row_send[at, :, 0, :] = out
        scatter(row_send.at[at], row_recv.at[at], row_ssem.at[at], row_rsem.at[at], -1)
        row_recv[at, 0] = row_send[at, 0]
        got = wait_rows(at)
        turned = pltpu.roll(got, half, 1)
        both = jnp.concatenate(
            [jnp.where(left, got, turned), jnp.where(left, turned, got)], axis=0)
        spend = vdup[...] * pick(hit_t[...], both)
        duals = jnp.maximum(
            0.0, lam[...] + temper * jnp.log((spend + limit) / (2.0 * limit)))
        lam[...] = duals
        vdup[...] = weights_of(duals)
        send_weights(at + 1)

    sweep(0, wait_rows(0))
    sweep(1, wait_rows(2))
    dual_send[...] = lam[...]
    swap_duals = remote(dual_send, dual_recv, dual_ssem, dual_rsem, (me, 1 - rep))
    swap_duals.start()
    den = denominator(2, wait_rows(4))
    result = jnp.where(live_users, temper * jnp.log(den), 0.0)
    user_out[...] = jnp.where(rep == 0, result[:, :half_users], result[:, half_users:])
    swap_duals.wait()
    dual_out[...] = jnp.where(left == (rep == 0), dual_send[...], dual_recv[...])


def body(
    user_emb, elig_owner, elig_local, cluster_size, camp_emb, camp_count, dual_init, spend_limit
):
    n = lax.axis_size("shard")
    radix = round(n ** (1 / 3))
    clusters, user_slots, width = user_emb.shape
    blocks, block_camps, _ = camp_emb.shape
    fan = elig_owner.shape[1]
    half = block_camps // 2
    vmem = pl.BlockSpec(memory_space=pltpu.VMEM)
    hbm = pl.BlockSpec(memory_space=pl.ANY)
    bf, f32, i32 = jnp.bfloat16, jnp.float32, jnp.int32
    dma = pltpu.SemaphoreType.DMA
    all_users = 2 * user_slots
    return pl.pallas_call(
        functools.partial(kernel, radix),
        out_shape=(
            jax.ShapeDtypeStruct((clusters, user_slots), f32),
            jax.ShapeDtypeStruct((blocks, block_camps), f32),
        ),
        in_specs=[vmem] * 6 + [hbm] * 2,
        out_specs=(vmem, vmem),
        scratch_shapes=[
            pltpu.VMEM((blocks, half, width), bf),
            pltpu.VMEM((clusters, all_users, width), bf),
            pltpu.VMEM((clusters, all_users, 128), f32),
            pltpu.VMEM((2 * n, half, width), bf),
            pltpu.VMEM((2 * n, half, width), bf),
            pltpu.VMEM((clusters, all_users, fan * half), bf),
            pltpu.VMEM((8, 128), i32),
            pltpu.VMEM((n, 1, 128), i32),
            pltpu.VMEM((1, 128), i32),
            pltpu.SMEM((1, 128), i32),
            pltpu.VMEM((n, 1, 128), i32),
            pltpu.SMEM((n, 1, 128), i32),
            pltpu.VMEM((n, 128), bf),
            pltpu.VMEM((128, n), bf),
            pltpu.VMEM((5, n, 1, block_camps), f32),
            pltpu.VMEM((5, n, 1, block_camps), f32),
            pltpu.VMEM((3, clusters, all_users), f32),
            pltpu.VMEM((3, clusters, all_users), f32),
            pltpu.VMEM((blocks, block_camps), f32),
            pltpu.VMEM((blocks, block_camps), f32),
            pltpu.VMEM((2 * n, blocks), bf),
            pltpu.VMEM((blocks, 2 * n), bf),
            pltpu.VMEM((blocks, block_camps), f32),
            pltpu.VMEM((blocks, block_camps), f32),
            dma, dma, dma, dma, dma, dma, dma, dma, dma, dma,
            dma((5,)), dma((5,)), dma((3,)), dma((3,)), dma, dma,
        ],
        compiler_params=pltpu.CompilerParams(
            collective_id=0, has_side_effects=True, vmem_limit_bytes=56 << 20
        ),
        name="allocate",
    )(
        elig_owner.T, elig_local.T, cluster_size.reshape(1, clusters),
        camp_count.reshape(1, blocks), dual_init, spend_limit, camp_emb, user_emb,
    )


def solution(mesh):
    return jax.shard_map(
        body,
        mesh=mesh,
        in_specs=(
            P("shard", "rep", None),
            P("shard", None),
            P("shard", None),
            P("shard"),
            P("shard", None, None),
            P("shard"),
            P("shard", None),
            P("shard", None),
        ),
        out_specs=(P("shard", "rep"), P("shard", None)),
        check_vma=False,
    )
```

```python
import functools
import math

import jax
import jax.numpy as jnp
from jax import lax
from jax.experimental import pallas as pl
from jax.experimental.pallas import tpu as pltpu
from jax.sharding import PartitionSpec as P

epsilon = 1e-06
temper = 0.25
sharpness = 16.0
mix = 37
MESH = pl.DeviceIdType.MESH


def kernel(
    radix,
    owner_ref,
    local_ref,
    size_ref,
    count_ref,
    dual_init,
    limits,
    camp_hbm,
    user_hbm,
    user_out,
    dual_out,
    camps,
    users,
    user_scale,
    sendbuf,
    recvbuf,
    kmat,
    rows_pad,
    wanted,
    slots,
    slots_smem,
    ids_in,
    ids_smem,
    to_slots,
    to_items,
    row_send,
    row_recv,
    den_send,
    den_recv,
    last_send,
    last_recv,
    dual_send,
    dual_recv,
    hit,
    hit_t,
    lam,
    vdup,
    camp_sem,
    user_sem,
    smem_sem,
    slot_sem,
    user_ssem,
    user_rsem,
    ids_ssem,
    ids_rsem,
    bulk_ssem,
    bulk_rsem,
    row_ssem,
    row_rsem,
    den_ssem,
    den_rsem,
    dual_ssem,
    dual_rsem,
):
    me = lax.axis_index("shard")
    rep = lax.axis_index("rep")
    n = wanted.shape[0]
    clusters, half_users, width = user_hbm.shape
    all_users = 2 * half_users
    half = camps.shape[1]
    lanes = 2 * half
    blocks = camps.shape[0]

    my_rows = pl.ds(pl.multiple_of(rep * half, half), half)
    my_users = pl.ds(pl.multiple_of(rep * half_users, half_users), half_users)
    load_camps = pltpu.make_async_copy(camp_hbm.at[:, my_rows, :], camps, camp_sem)
    load_camps.start()
    load_users = pltpu.make_async_copy(user_hbm, users.at[:, my_users, :], user_sem)
    load_users.start()

    places = (radix * radix, radix, 1)
    digits = [(me // p) % radix for p in places]
    moved = {
        sign: [
            [((digit + sign * j + radix) % radix) * p for j in range(radix)]
            for digit, p in zip(digits, places)
        ]
        for sign in (1, -1)
    }

    def partner(d, sign):
        return sum(moved[sign][i][(d // p) % radix] for i, p in enumerate(places))

    def hops(d):
        steps = [(d // p) % radix for p in places]
        return sum(min(t, radix - t) for t in steps)

    order = [(i * mix) % n for i in range(1, n)]

    def hops(d):
        steps = [(d // p) % radix for p in places]
        return sum(min(t, radix - t) for t in steps)

    bulk_order = sorted(order, key=lambda d: hops(d) <= 1)
    order = sorted(order, key=lambda d: -hops(d))

    barrier = pltpu.get_barrier_semaphore()
    for d in order:
        pl.semaphore_signal(
            barrier, inc=1, device_id=(partner(d, 1), rep), device_id_type=MESH
        )
    pl.semaphore_signal(barrier, inc=1, device_id=(me, 1 - rep), device_id_type=MESH)

    def remote(src, dst, ssem, rsem, target):
        return pltpu.make_async_remote_copy(
            src_ref=src, dst_ref=dst, send_sem=ssem, recv_sem=rsem,
            device_id=target, device_id_type=MESH,
        )

    def scatter(src, dst, ssem, rsem, sign):
        for d in order:
            remote(src.at[d], dst.at[d], ssem, rsem, (partner(d, sign), rep)).start()

    def all_of(src, dst, ssem, rsem):
        rest = pl.ds(1, n - 1)
        return remote(src.at[rest], dst.at[rest], ssem, rsem, (me, 1 - rep))

    fan, _ = owner_ref.shape
    i32, f32, bf16 = jnp.int32, jnp.float32, jnp.bfloat16
    lane = lax.broadcasted_iota(i32, (1, lanes), 1)
    left = lane < half
    evens, odds = list(range(0, fan, 2)), list(range(1, fan, 2))
    columns = evens + odds + odds + evens

    def column_row(ref):
        rows_pad[...] = jnp.zeros_like(rows_pad)
        rows_pad[0:fan, 0:clusters] = ref[...]
        row = rows_pad[...]
        out = jnp.zeros((1, lanes), i32)
        for at, e in enumerate(columns):
            piece = row[e:e + 1]
            out = out + (pltpu.roll(piece, at * clusters, 1) if at else piece)
        return out

    owner = column_row(owner_ref)
    local = column_row(local_ref)
    dist = jnp.zeros_like(owner)
    shift = radix.bit_length() - 1
    for i, p in enumerate(places):
        digit = lax.shift_right_logical(owner, i32(p.bit_length() - 1)) & (radix - 1)
        dist = dist + ((digits[i] - digit + radix) & (radix - 1)) * p
    mask = dist == lax.broadcasted_iota(i32, (n, lanes), 0)
    from_col = lax.broadcasted_iota(i32, (lanes, lanes), 0)
    to_col = lax.broadcasted_iota(i32, (lanes, lanes), 1)
    cluster_of = clusters - 1
    ahead = (from_col < half) & ((from_col & cluster_of) < (to_col & cluster_of))
    prefix = jnp.dot(
        mask.astype(f32).astype(bf16), ahead.astype(f32).astype(bf16),
        preferred_element_type=f32)
    rank = (lane >= half).astype(i32)
    chosen = mask & (prefix == rank.astype(f32))
    to_slots[...] = chosen.astype(f32).astype(bf16)
    to_items[...] = chosen.astype(f32).T.astype(bf16)
    first = jnp.sum(jnp.where(chosen & left, local, 0), axis=1, keepdims=True)
    second = jnp.sum(jnp.where(chosen & ~left, local, 0), axis=1, keepdims=True)
    wanted[:, 0, :] = jnp.where(lane == 0, first, second)
    slot = lax.broadcasted_iota(i32, (n, lanes), 0) * 2 + rank
    slots[...] = jnp.sum(jnp.where(chosen, slot, 0), axis=0, keepdims=True)
    slots_to_smem = pltpu.make_async_copy(slots, slots_smem, slot_sem)
    slots_to_smem.start()

    pl.semaphore_wait(barrier, n)

    scatter(wanted, ids_in, ids_ssem, ids_rsem, -1)
    swap_users = remote(
        user_hbm, users.at[:, my_users, :], user_ssem, user_rsem, (me, 1 - rep)
    )
    swap_users.start()
    ids_in[0] = wanted[0]

    def spread(x):
        rolled = pltpu.roll(x, half, 1)
        mine = left == (rep == 0)
        return jnp.where(mine, x, rolled)

    lam[...] = spread(dual_init[...])
    limit = spread(limits[...])
    diagonal = from_col == to_col

    def column(row):
        return jnp.sum(jnp.where(diagonal[:blocks], row.astype(f32), 0.0), axis=1, keepdims=True)

    counts = column(count_ref[...])
    camp_pos = jnp.where(left, lane, lane - half) + rep * half
    live_camps = camp_pos.astype(f32) < counts

    def weights_of(duals):
        return jnp.where(live_camps, jnp.exp(duals * (-1.0 / temper)), 0.0)

    vdup[...] = weights_of(lam[...])

    all_of(wanted, ids_in, ids_ssem, ids_rsem).wait()
    to_smem = pltpu.make_async_copy(ids_in, ids_smem, smem_sem)
    to_smem.start()
    ids = ids_in[:, 0, :]
    block_ids = lax.broadcasted_iota(jnp.int32, (n, blocks), 1)
    hits = jnp.concatenate(
        [(jnp.broadcast_to(ids[:, j:j + 1], (n, blocks)) == block_ids).astype(f32)
         for j in range(2)], axis=0)
    hit[...] = hits.astype(bf16)
    hit_t[...] = hits.T.astype(bf16)

    def pick(table, x):
        upper = x.astype(bf16)
        lower = (x - upper.astype(f32)).astype(bf16)
        out = jnp.dot(
            table, jnp.concatenate([upper, lower], axis=1), preferred_element_type=f32)
        return out[:, :lanes] + out[:, lanes:]

    def send_weights(step):
        picked = pick(hit[...], vdup[...])
        row_send[step, :, 0, :] = jnp.where(left, picked[:n], picked[n:])
        scatter(row_send.at[step], row_recv.at[step], row_ssem.at[step], row_rsem.at[step], 1)
        row_recv[step, 0] = row_send[step, 0]

    def wait_rows(step):
        all_of(
            row_send.at[step], row_recv.at[step], row_ssem.at[step], row_rsem.at[step]
        ).wait()
        return row_recv[step, :, 0, :]

    to_smem.wait()
    load_camps.wait()

    def clamp(i, size):
        return jnp.minimum(jnp.maximum(i, 0), size - 1)

    for d in bulk_order:
        for j in range(2):
            sendbuf[2 * d + j] = camps[clamp(ids_smem[d, 0, j], blocks)]
        pair = pl.ds(2 * d, 2)
        remote(
            sendbuf.at[pair], recvbuf.at[pair], bulk_ssem, bulk_rsem, (partner(d, 1), rep)
        ).start()

    for j in range(2):
        recvbuf[j] = camps[clamp(ids_smem[0, 0, j], blocks)]

    send_weights(0)
    load_users.wait()
    swap_users.wait()

    chunk = 256 if all_users % 256 == 0 else all_users
    chunks = all_users // chunk

    @pl.loop(0, clusters * chunks)
    def _(i):
        k = i // chunks
        at = pl.ds(pl.multiple_of((i % chunks) * chunk, chunk), chunk)
        x = users[k, at, :].astype(jnp.float32)
        mean = jnp.sum(x * x, axis=1, keepdims=True) * (1.0 / width)
        user_scale[k, at, :] = jnp.broadcast_to(lax.rsqrt(mean + epsilon), (chunk, 128))

    rest = pl.ds(2, 2 * n - 2)
    remote(sendbuf.at[rest], recvbuf.at[rest], bulk_ssem, bulk_rsem, (me, 1 - rep)).wait()

    factor = sharpness / width / temper * math.log2(math.e)
    cols = fan * half

    slots_to_smem.wait()
    first_at = [columns.index(e) * clusters for e in range(fan)]
    second_at = [(columns.index(e, fan)) * clusters for e in range(fan)]

    @pl.loop(0, clusters, unroll=4)
    def _(k):
        emb = jnp.concatenate(
            [recvbuf[clamp(
                slots_smem[0, first_at[e] + k] + slots_smem[0, second_at[e] + k], 2 * n)]
             for e in range(fan)], axis=0)
        wide = emb.astype(jnp.float32)
        square = wide * wide
        upper = square.astype(jnp.bfloat16)
        lower = (square - upper.astype(jnp.float32)).astype(jnp.bfloat16)
        ones = jnp.ones((16, width), jnp.bfloat16)
        dims = (((1,), (1,)), ((), ()))
        total = lax.dot_general(ones, upper, dims, preferred_element_type=jnp.float32)
        total = total + lax.dot_general(ones, lower, dims, preferred_element_type=jnp.float32)
        camp_scale = lax.rsqrt(total[0:1] * (1.0 / width) + epsilon) * factor
        for c in range(chunks):
            at = pl.ds(c * chunk, chunk)
            raw = lax.dot_general(users[k, at, :], emb, dims, preferred_element_type=jnp.float32)
            scale = user_scale[k, at, :]
            wide_scale = jnp.concatenate([scale] * (cols // 128), axis=1)
            kmat[k, at, :] = jnp.exp2(raw * wide_scale * camp_scale).astype(jnp.bfloat16)

    def split(x):
        upper = x.astype(jnp.bfloat16)
        lower = (x - upper.astype(jnp.float32)).astype(jnp.bfloat16)
        return jnp.concatenate([upper, lower], axis=0)

    part = fan * clusters // 2
    group = clusters // 2
    row_id = lax.broadcasted_iota(i32, (group, 1), 0)

    sizes = jnp.sum(
        jnp.where(diagonal[:clusters, :clusters], size_ref[...].astype(f32), 0.0),
        axis=1, keepdims=True).astype(i32)
    live_users = lax.broadcasted_iota(i32, (clusters, all_users), 1) < sizes

    def item_weights(rows):
        picked = pick(to_items[...], rows)
        a, b, c, d = [picked[p * part:(p + 1) * part] for p in range(4)]
        table = jnp.where(left, a + pltpu.roll(d, half, 1), c + pltpu.roll(b, half, 1))
        return split(jnp.concatenate(
            [table[p * clusters:(p + 1) * clusters] for p in range(fan // 2)], axis=1))

    def partial_sums(v, h):
        at = h * group

        def add(k, acc):
            out = lax.dot_general(
                v, kmat[k], (((1,), (1,)), ((), ())), preferred_element_type=f32)
            both = out[at:at + group] + out[clusters + at:clusters + at + group]
            return acc + jnp.where(row_id == k - at, both, 0.0)

        zero = jnp.zeros((group, all_users), f32)
        return lax.fori_loop(at, at + group, add, zero, unroll=4)

    def sweep(step, rows):
        v = item_weights(rows)
        own, swaps, sums = [], [], []
        for h in range(2):
            own.append(partial_sums(v, h))
            at = pl.ds(h * group, group)
            den_send[step, at] = own[h]
            swaps.append(remote(
                den_send.at[step, at], den_recv.at[step, at],
                den_ssem.at[2 * step + h], den_rsem.at[2 * step + h], (me, 1 - rep)))
            swaps[h].start()
        for h in range(2):
            at = h * group
            swaps[h].wait()
            den = 1.0 + (own[h] + den_recv[step, at:at + group])
            q = jnp.where(live_users[at:at + group], 1.0 / den, 0.0)
            upper = q.astype(bf16).astype(f32)
            q = jnp.concatenate([upper, q - upper], axis=0).astype(bf16)

            def add(k, acc, q=q, at=at):
                out = jnp.dot(q, kmat[k], preferred_element_type=f32)
                return acc + jnp.where(row_id == k - at, out[:group] + out[group:], 0.0)

            sums.append(lax.fori_loop(
                at, at + group, add, jnp.zeros((group, cols), f32), unroll=4))
        sums = jnp.concatenate(sums, axis=0)
        table = jnp.concatenate(
            [sums[:, p * lanes:(p + 1) * lanes] for p in range(fan // 2)], axis=0)
        rolled = pltpu.roll(table, half, 1)
        zero = jnp.zeros_like(table)
        stack = jnp.concatenate(
            [jnp.where(left, table, zero), jnp.where(left, rolled, zero),
             jnp.where(left, zero, table), jnp.where(left, zero, rolled)], axis=0)
        out = pick(to_slots[...], stack)
        at = 2 * step + 1
        row_send[at, :, 0, :] = out
        scatter(row_send.at[at], row_recv.at[at], row_ssem.at[at], row_rsem.at[at], -1)
        row_recv[at, 0] = row_send[at, 0]
        got = wait_rows(at)
        turned = pltpu.roll(got, half, 1)
        both = jnp.concatenate(
            [jnp.where(left, got, turned), jnp.where(left, turned, got)], axis=0)
        spend = vdup[...] * pick(hit_t[...], both)
        duals = jnp.maximum(
            0.0, lam[...] + temper * jnp.log((spend + limit) / (2.0 * limit)))
        lam[...] = duals
        vdup[...] = weights_of(duals)
        send_weights(at + 1)

    sweep(0, wait_rows(0))
    sweep(1, wait_rows(2))
    dual_send[...] = lam[...]
    swap_duals = remote(dual_send, dual_recv, dual_ssem, dual_rsem, (me, 1 - rep))
    swap_duals.start()
    v = item_weights(wait_rows(4))
    mine, swaps = [], []
    for h in range(2):
        own = partial_sums(v, h)
        low, high = own[:, :half_users], own[:, half_users:]
        mine.append(jnp.where(rep == 0, low, high))
        at = pl.ds(h * group, group)
        last_send[at] = jnp.where(rep == 0, high, low)
        swaps.append(remote(
            last_send.at[at], last_recv.at[at], den_ssem.at[4 + h], den_rsem.at[4 + h],
            (me, 1 - rep)))
        swaps[h].start()
    user_pos = lax.broadcasted_iota(i32, (clusters, half_users), 1) + rep * half_users
    for h in range(2):
        at = h * group
        swaps[h].wait()
        den = 1.0 + (mine[h] + last_recv[at:at + group])
        user_out[at:at + group] = jnp.where(
            user_pos[at:at + group] < sizes[at:at + group], temper * jnp.log(den), 0.0)
    swap_duals.wait()
    dual_out[...] = jnp.where(left == (rep == 0), dual_send[...], dual_recv[...])


def body(
    user_emb, elig_owner, elig_local, cluster_size, camp_emb, camp_count, dual_init, spend_limit
):
    n = lax.axis_size("shard")
    radix = round(n ** (1 / 3))
    clusters, user_slots, width = user_emb.shape
    blocks, block_camps, _ = camp_emb.shape
    fan = elig_owner.shape[1]
    half = block_camps // 2
    vmem = pl.BlockSpec(memory_space=pltpu.VMEM)
    hbm = pl.BlockSpec(memory_space=pl.ANY)
    bf, f32, i32 = jnp.bfloat16, jnp.float32, jnp.int32
    dma = pltpu.SemaphoreType.DMA
    all_users = 2 * user_slots
    return pl.pallas_call(
        functools.partial(kernel, radix),
        out_shape=(
            jax.ShapeDtypeStruct((clusters, user_slots), f32),
            jax.ShapeDtypeStruct((blocks, block_camps), f32),
        ),
        in_specs=[vmem] * 6 + [hbm] * 2,
        out_specs=(vmem, vmem),
        scratch_shapes=[
            pltpu.VMEM((blocks, half, width), bf),
            pltpu.VMEM((clusters, all_users, width), bf),
            pltpu.VMEM((clusters, all_users, 128), f32),
            pltpu.VMEM((2 * n, half, width), bf),
            pltpu.VMEM((2 * n, half, width), bf),
            pltpu.VMEM((clusters, all_users, fan * half), bf),
            pltpu.VMEM((8, 128), i32),
            pltpu.VMEM((n, 1, 128), i32),
            pltpu.VMEM((1, 128), i32),
            pltpu.SMEM((1, 128), i32),
            pltpu.VMEM((n, 1, 128), i32),
            pltpu.SMEM((n, 1, 128), i32),
            pltpu.VMEM((n, 128), bf),
            pltpu.VMEM((128, n), bf),
            pltpu.VMEM((5, n, 1, block_camps), f32),
            pltpu.VMEM((5, n, 1, block_camps), f32),
            pltpu.VMEM((2, clusters, all_users), f32),
            pltpu.VMEM((2, clusters, all_users), f32),
            pltpu.VMEM((clusters, user_slots), f32),
            pltpu.VMEM((clusters, user_slots), f32),
            pltpu.VMEM((blocks, block_camps), f32),
            pltpu.VMEM((blocks, block_camps), f32),
            pltpu.VMEM((2 * n, blocks), bf),
            pltpu.VMEM((blocks, 2 * n), bf),
            pltpu.VMEM((blocks, block_camps), f32),
            pltpu.VMEM((blocks, block_camps), f32),
            dma, dma, dma, dma, dma, dma, dma, dma, dma, dma,
            dma((5,)), dma((5,)), dma((6,)), dma((6,)), dma, dma,
        ],
        compiler_params=pltpu.CompilerParams(
            collective_id=0, has_side_effects=True, vmem_limit_bytes=56 << 20
        ),
        name="allocate",
    )(
        elig_owner.T, elig_local.T, cluster_size.reshape(1, clusters),
        camp_count.reshape(1, blocks), dual_init, spend_limit, camp_emb, user_emb,
    )


def solution(mesh):
    return jax.shard_map(
        body,
        mesh=mesh,
        in_specs=(
            P("shard", "rep", None),
            P("shard", None),
            P("shard", None),
            P("shard"),
            P("shard", None, None),
            P("shard"),
            P("shard", None),
            P("shard", None),
        ),
        out_specs=(P("shard", "rep"), P("shard", None)),
        check_vma=False,
    )
```

```python
import functools
import math

import jax
import jax.numpy as jnp
from jax import lax
from jax.experimental import pallas as pl
from jax.experimental.pallas import tpu as pltpu
from jax.sharding import PartitionSpec as P

epsilon = 1e-06
temper = 0.25
sharpness = 16.0
mix = 37
MESH = pl.DeviceIdType.MESH


def kernel(
    radix,
    owner_hbm,
    local_hbm,
    size_hbm,
    count_hbm,
    init_hbm,
    limit_hbm,
    camp_hbm,
    user_hbm,
    user_out_hbm,
    dual_out_hbm,
    owner_ref,
    local_ref,
    size_ref,
    count_ref,
    dual_init,
    limits,
    user_out,
    dual_out,
    camps,
    users,
    user_scale,
    sendbuf,
    recvbuf,
    kmat,
    rows_pad,
    wanted,
    slots,
    slots_smem,
    ids_in,
    ids_smem,
    to_slots,
    to_items,
    row_send,
    row_recv,
    den_send,
    den_recv,
    last_send,
    last_recv,
    dual_send,
    dual_recv,
    hit,
    hit_t,
    lam,
    vdup,
    small_sem,
    out_sem,
    camp_sem,
    user_sem,
    smem_sem,
    slot_sem,
    user_ssem,
    user_rsem,
    ids_ssem,
    ids_rsem,
    bulk_ssem,
    bulk_rsem,
    row_ssem,
    row_rsem,
    den_ssem,
    den_rsem,
    dual_ssem,
    dual_rsem,
):
    me = lax.axis_index("shard")
    rep = lax.axis_index("rep")
    n = wanted.shape[0]
    clusters, half_users, width = user_hbm.shape
    all_users = 2 * half_users
    half = camps.shape[1]
    lanes = 2 * half
    blocks = camps.shape[0]

    places = (radix * radix, radix, 1)
    digits = [(me // p) % radix for p in places]
    moved = {
        sign: [
            [((digit + sign * j + radix) % radix) * p for j in range(radix)]
            for digit, p in zip(digits, places)
        ]
        for sign in (1, -1)
    }

    def partner(d, sign):
        return sum(moved[sign][i][(d // p) % radix] for i, p in enumerate(places))

    def hops(d):
        steps = [(d // p) % radix for p in places]
        return sum(min(t, radix - t) for t in steps)

    order = [(i * mix) % n for i in range(1, n)]

    def hops(d):
        steps = [(d // p) % radix for p in places]
        return sum(min(t, radix - t) for t in steps)

    bulk_order = sorted(order, key=lambda d: hops(d) <= 1)
    order = sorted(order, key=lambda d: -hops(d))

    barrier = pltpu.get_barrier_semaphore()
    for d in order:
        pl.semaphore_signal(
            barrier, inc=1, device_id=(partner(d, 1), rep), device_id_type=MESH
        )
    pl.semaphore_signal(barrier, inc=1, device_id=(me, 1 - rep), device_id_type=MESH)

    def fetch(src, dst, i):
        copy = pltpu.make_async_copy(src, dst, small_sem.at[i])
        copy.start()
        return copy

    get_owner = fetch(owner_hbm, owner_ref, 0)
    get_local = fetch(local_hbm, local_ref, 1)
    get_rest = [
        fetch(size_hbm, size_ref, 2), fetch(count_hbm, count_ref, 3),
        fetch(init_hbm, dual_init, 4), fetch(limit_hbm, limits, 5),
    ]
    my_rows = pl.ds(pl.multiple_of(rep * half, half), half)
    my_users = pl.ds(pl.multiple_of(rep * half_users, half_users), half_users)
    load_camps = pltpu.make_async_copy(camp_hbm.at[:, my_rows, :], camps, camp_sem)
    load_camps.start()
    load_users = pltpu.make_async_copy(user_hbm, users.at[:, my_users, :], user_sem)
    load_users.start()

    def remote(src, dst, ssem, rsem, target):
        return pltpu.make_async_remote_copy(
            src_ref=src, dst_ref=dst, send_sem=ssem, recv_sem=rsem,
            device_id=target, device_id_type=MESH,
        )

    def scatter(src, dst, ssem, rsem, sign):
        for d in order:
            remote(src.at[d], dst.at[d], ssem, rsem, (partner(d, sign), rep)).start()

    def all_of(src, dst, ssem, rsem):
        rest = pl.ds(1, n - 1)
        return remote(src.at[rest], dst.at[rest], ssem, rsem, (me, 1 - rep))

    fan, _ = owner_ref.shape
    i32, f32, bf16 = jnp.int32, jnp.float32, jnp.bfloat16
    lane = lax.broadcasted_iota(i32, (1, lanes), 1)
    left = lane < half
    evens, odds = list(range(0, fan, 2)), list(range(1, fan, 2))
    columns = evens + odds + odds + evens

    def column_row(ref):
        rows_pad[...] = jnp.zeros_like(rows_pad)
        rows_pad[0:fan, 0:clusters] = ref[...]
        row = rows_pad[...]
        out = jnp.zeros((1, lanes), i32)
        for at, e in enumerate(columns):
            piece = row[e:e + 1]
            out = out + (pltpu.roll(piece, at * clusters, 1) if at else piece)
        return out

    get_owner.wait()
    get_local.wait()
    owner = column_row(owner_ref)
    local = column_row(local_ref)
    dist = jnp.zeros_like(owner)
    shift = radix.bit_length() - 1
    for i, p in enumerate(places):
        digit = lax.shift_right_logical(owner, i32(p.bit_length() - 1)) & (radix - 1)
        dist = dist + ((digits[i] - digit + radix) & (radix - 1)) * p
    mask = dist == lax.broadcasted_iota(i32, (n, lanes), 0)
    from_col = lax.broadcasted_iota(i32, (lanes, lanes), 0)
    to_col = lax.broadcasted_iota(i32, (lanes, lanes), 1)
    cluster_of = clusters - 1
    ahead = (from_col < half) & ((from_col & cluster_of) < (to_col & cluster_of))
    prefix = jnp.dot(
        mask.astype(f32).astype(bf16), ahead.astype(f32).astype(bf16),
        preferred_element_type=f32)
    rank = (lane >= half).astype(i32)
    chosen = mask & (prefix == rank.astype(f32))
    to_slots[...] = chosen.astype(f32).astype(bf16)
    to_items[...] = chosen.astype(f32).T.astype(bf16)
    first = jnp.sum(jnp.where(chosen & left, local, 0), axis=1, keepdims=True)
    second = jnp.sum(jnp.where(chosen & ~left, local, 0), axis=1, keepdims=True)
    wanted[:, 0, :] = jnp.where(lane == 0, first, second)
    slot = lax.broadcasted_iota(i32, (n, lanes), 0) * 2 + rank
    slots[...] = jnp.sum(jnp.where(chosen, slot, 0), axis=0, keepdims=True)
    slots_to_smem = pltpu.make_async_copy(slots, slots_smem, slot_sem)
    slots_to_smem.start()

    pl.semaphore_wait(barrier, n)

    scatter(wanted, ids_in, ids_ssem, ids_rsem, -1)
    swap_users = remote(
        user_hbm, users.at[:, my_users, :], user_ssem, user_rsem, (me, 1 - rep)
    )
    swap_users.start()
    ids_in[0] = wanted[0]

    def spread(x):
        rolled = pltpu.roll(x, half, 1)
        mine = left == (rep == 0)
        return jnp.where(mine, x, rolled)

    for copy in get_rest:
        copy.wait()
    lam[...] = spread(dual_init[...])
    limit = spread(limits[...])
    diagonal = from_col == to_col

    def column(row):
        return jnp.sum(jnp.where(diagonal[:blocks], row.astype(f32), 0.0), axis=1, keepdims=True)

    counts = column(count_ref[...])
    camp_pos = jnp.where(left, lane, lane - half) + rep * half
    live_camps = camp_pos.astype(f32) < counts

    def weights_of(duals):
        return jnp.where(live_camps, jnp.exp(duals * (-1.0 / temper)), 0.0)

    vdup[...] = weights_of(lam[...])

    all_of(wanted, ids_in, ids_ssem, ids_rsem).wait()
    to_smem = pltpu.make_async_copy(ids_in, ids_smem, smem_sem)
    to_smem.start()
    ids = ids_in[:, 0, :]
    block_ids = lax.broadcasted_iota(jnp.int32, (n, blocks), 1)
    hits = jnp.concatenate(
        [(jnp.broadcast_to(ids[:, j:j + 1], (n, blocks)) == block_ids).astype(f32)
         for j in range(2)], axis=0)
    hit[...] = hits.astype(bf16)
    hit_t[...] = hits.T.astype(bf16)

    def pick(table, x):
        upper = x.astype(bf16)
        lower = (x - upper.astype(f32)).astype(bf16)
        out = jnp.dot(
            table, jnp.concatenate([upper, lower], axis=1), preferred_element_type=f32)
        return out[:, :lanes] + out[:, lanes:]

    def send_weights(step):
        picked = pick(hit[...], vdup[...])
        row_send[step, :, 0, :] = jnp.where(left, picked[:n], picked[n:])
        scatter(row_send.at[step], row_recv.at[step], row_ssem.at[step], row_rsem.at[step], 1)
        row_recv[step, 0] = row_send[step, 0]

    def wait_rows(step):
        all_of(
            row_send.at[step], row_recv.at[step], row_ssem.at[step], row_rsem.at[step]
        ).wait()
        return row_recv[step, :, 0, :]

    to_smem.wait()
    load_camps.wait()

    def clamp(i, size):
        return jnp.minimum(jnp.maximum(i, 0), size - 1)

    for d in bulk_order:
        for j in range(2):
            sendbuf[2 * d + j] = camps[clamp(ids_smem[d, 0, j], blocks)]
        pair = pl.ds(2 * d, 2)
        remote(
            sendbuf.at[pair], recvbuf.at[pair], bulk_ssem, bulk_rsem, (partner(d, 1), rep)
        ).start()

    for j in range(2):
        recvbuf[j] = camps[clamp(ids_smem[0, 0, j], blocks)]

    send_weights(0)
    load_users.wait()
    swap_users.wait()

    chunk = 256 if all_users % 256 == 0 else all_users
    chunks = all_users // chunk

    @pl.loop(0, clusters * chunks)
    def _(i):
        k = i // chunks
        at = pl.ds(pl.multiple_of((i % chunks) * chunk, chunk), chunk)
        x = users[k, at, :].astype(jnp.float32)
        mean = jnp.sum(x * x, axis=1, keepdims=True) * (1.0 / width)
        user_scale[k, at, :] = jnp.broadcast_to(lax.rsqrt(mean + epsilon), (chunk, 128))

    rest = pl.ds(2, 2 * n - 2)
    remote(sendbuf.at[rest], recvbuf.at[rest], bulk_ssem, bulk_rsem, (me, 1 - rep)).wait()

    factor = sharpness / width / temper * math.log2(math.e)
    cols = fan * half

    slots_to_smem.wait()
    first_at = [columns.index(e) * clusters for e in range(fan)]
    second_at = [(columns.index(e, fan)) * clusters for e in range(fan)]

    @pl.loop(0, clusters, unroll=4)
    def _(k):
        emb = jnp.concatenate(
            [recvbuf[clamp(
                slots_smem[0, first_at[e] + k] + slots_smem[0, second_at[e] + k], 2 * n)]
             for e in range(fan)], axis=0)
        wide = emb.astype(jnp.float32)
        square = wide * wide
        upper = square.astype(jnp.bfloat16)
        lower = (square - upper.astype(jnp.float32)).astype(jnp.bfloat16)
        ones = jnp.ones((16, width), jnp.bfloat16)
        dims = (((1,), (1,)), ((), ()))
        total = lax.dot_general(ones, upper, dims, preferred_element_type=jnp.float32)
        total = total + lax.dot_general(ones, lower, dims, preferred_element_type=jnp.float32)
        camp_scale = lax.rsqrt(total[0:1] * (1.0 / width) + epsilon) * factor
        for c in range(chunks):
            at = pl.ds(c * chunk, chunk)
            raw = lax.dot_general(users[k, at, :], emb, dims, preferred_element_type=jnp.float32)
            scale = user_scale[k, at, :]
            wide_scale = jnp.concatenate([scale] * (cols // 128), axis=1)
            kmat[k, at, :] = jnp.exp2(raw * wide_scale * camp_scale).astype(jnp.bfloat16)

    def split(x):
        upper = x.astype(jnp.bfloat16)
        lower = (x - upper.astype(jnp.float32)).astype(jnp.bfloat16)
        return jnp.concatenate([upper, lower], axis=0)

    part = fan * clusters // 2
    group = clusters // 2
    row_id = lax.broadcasted_iota(i32, (group, 1), 0)

    sizes = jnp.sum(
        jnp.where(diagonal[:clusters, :clusters], size_ref[...].astype(f32), 0.0),
        axis=1, keepdims=True).astype(i32)
    live_users = lax.broadcasted_iota(i32, (clusters, all_users), 1) < sizes

    def item_weights(rows):
        picked = pick(to_items[...], rows)
        a, b, c, d = [picked[p * part:(p + 1) * part] for p in range(4)]
        table = jnp.where(left, a + pltpu.roll(d, half, 1), c + pltpu.roll(b, half, 1))
        return split(jnp.concatenate(
            [table[p * clusters:(p + 1) * clusters] for p in range(fan // 2)], axis=1))

    def partial_sums(v, h):
        at = h * group

        def add(k, acc):
            out = lax.dot_general(
                v, kmat[k], (((1,), (1,)), ((), ())), preferred_element_type=f32)
            both = out[at:at + group] + out[clusters + at:clusters + at + group]
            return acc + jnp.where(row_id == k - at, both, 0.0)

        zero = jnp.zeros((group, all_users), f32)
        return lax.fori_loop(at, at + group, add, zero, unroll=8)

    def sweep(step, rows):
        v = item_weights(rows)
        own, swaps, sums = [], [], []
        for h in range(2):
            own.append(partial_sums(v, h))
            at = pl.ds(h * group, group)
            den_send[step, at] = own[h]
            swaps.append(remote(
                den_send.at[step, at], den_recv.at[step, at],
                den_ssem.at[2 * step + h], den_rsem.at[2 * step + h], (me, 1 - rep)))
            swaps[h].start()
        for h in range(2):
            at = h * group
            swaps[h].wait()
            den = 1.0 + (own[h] + den_recv[step, at:at + group])
            q = jnp.where(live_users[at:at + group], 1.0 / den, 0.0)
            upper = q.astype(bf16).astype(f32)
            q = jnp.concatenate([upper, q - upper], axis=0).astype(bf16)

            def add(k, acc, q=q, at=at):
                out = jnp.dot(q, kmat[k], preferred_element_type=f32)
                return acc + jnp.where(row_id == k - at, out[:group] + out[group:], 0.0)

            sums.append(lax.fori_loop(
                at, at + group, add, jnp.zeros((group, cols), f32), unroll=8))
        sums = jnp.concatenate(sums, axis=0)
        table = jnp.concatenate(
            [sums[:, p * lanes:(p + 1) * lanes] for p in range(fan // 2)], axis=0)
        rolled = pltpu.roll(table, half, 1)
        zero = jnp.zeros_like(table)
        stack = jnp.concatenate(
            [jnp.where(left, table, zero), jnp.where(left, rolled, zero),
             jnp.where(left, zero, table), jnp.where(left, zero, rolled)], axis=0)
        out = pick(to_slots[...], stack)
        at = 2 * step + 1
        row_send[at, :, 0, :] = out
        scatter(row_send.at[at], row_recv.at[at], row_ssem.at[at], row_rsem.at[at], -1)
        row_recv[at, 0] = row_send[at, 0]
        got = wait_rows(at)
        turned = pltpu.roll(got, half, 1)
        both = jnp.concatenate(
            [jnp.where(left, got, turned), jnp.where(left, turned, got)], axis=0)
        spend = vdup[...] * pick(hit_t[...], both)
        duals = jnp.maximum(
            0.0, lam[...] + temper * jnp.log((spend + limit) / (2.0 * limit)))
        lam[...] = duals
        vdup[...] = weights_of(duals)
        send_weights(at + 1)

    sweep(0, wait_rows(0))
    sweep(1, wait_rows(2))
    dual_send[...] = lam[...]
    swap_duals = remote(dual_send, dual_recv, dual_ssem, dual_rsem, (me, 1 - rep))
    swap_duals.start()
    v = item_weights(wait_rows(4))
    mine, swaps = [], []
    for h in range(2):
        own = partial_sums(v, h)
        low, high = own[:, :half_users], own[:, half_users:]
        mine.append(jnp.where(rep == 0, low, high))
        at = pl.ds(h * group, group)
        last_send[at] = jnp.where(rep == 0, high, low)
        swaps.append(remote(
            last_send.at[at], last_recv.at[at], den_ssem.at[4 + h], den_rsem.at[4 + h],
            (me, 1 - rep)))
        swaps[h].start()
    swap_duals.wait()
    dual_out[...] = jnp.where(left == (rep == 0), dual_send[...], dual_recv[...])
    put_duals = pltpu.make_async_copy(dual_out, dual_out_hbm, out_sem.at[0])
    put_duals.start()
    user_pos = lax.broadcasted_iota(i32, (clusters, half_users), 1) + rep * half_users
    for h in range(2):
        at = h * group
        swaps[h].wait()
        den = 1.0 + (mine[h] + last_recv[at:at + group])
        user_out[at:at + group] = jnp.where(
            user_pos[at:at + group] < sizes[at:at + group], temper * jnp.log(den), 0.0)
    put_users = pltpu.make_async_copy(user_out, user_out_hbm, out_sem.at[1])
    put_users.start()
    put_duals.wait()
    put_users.wait()


def body(
    user_emb, elig_owner, elig_local, cluster_size, camp_emb, camp_count, dual_init, spend_limit
):
    n = lax.axis_size("shard")
    radix = round(n ** (1 / 3))
    clusters, user_slots, width = user_emb.shape
    blocks, block_camps, _ = camp_emb.shape
    fan = elig_owner.shape[1]
    half = block_camps // 2
    hbm = pl.BlockSpec(memory_space=pl.ANY)
    bf, f32, i32 = jnp.bfloat16, jnp.float32, jnp.int32
    dma = pltpu.SemaphoreType.DMA
    all_users = 2 * user_slots
    return pl.pallas_call(
        functools.partial(kernel, radix),
        out_shape=(
            jax.ShapeDtypeStruct((clusters, user_slots), f32),
            jax.ShapeDtypeStruct((blocks, block_camps), f32),
        ),
        in_specs=[hbm] * 8,
        out_specs=(hbm, hbm),
        scratch_shapes=[
            pltpu.VMEM((fan, clusters), i32),
            pltpu.VMEM((fan, clusters), i32),
            pltpu.VMEM((1, clusters), i32),
            pltpu.VMEM((1, blocks), i32),
            pltpu.VMEM((blocks, block_camps), f32),
            pltpu.VMEM((blocks, block_camps), f32),
            pltpu.VMEM((clusters, user_slots), f32),
            pltpu.VMEM((blocks, block_camps), f32),
            pltpu.VMEM((blocks, half, width), bf),
            pltpu.VMEM((clusters, all_users, width), bf),
            pltpu.VMEM((clusters, all_users, 128), f32),
            pltpu.VMEM((2 * n, half, width), bf),
            pltpu.VMEM((2 * n, half, width), bf),
            pltpu.VMEM((clusters, all_users, fan * half), bf),
            pltpu.VMEM((8, 128), i32),
            pltpu.VMEM((n, 1, 128), i32),
            pltpu.VMEM((1, 128), i32),
            pltpu.SMEM((1, 128), i32),
            pltpu.VMEM((n, 1, 128), i32),
            pltpu.SMEM((n, 1, 128), i32),
            pltpu.VMEM((n, 128), bf),
            pltpu.VMEM((128, n), bf),
            pltpu.VMEM((5, n, 1, block_camps), f32),
            pltpu.VMEM((5, n, 1, block_camps), f32),
            pltpu.VMEM((2, clusters, all_users), f32),
            pltpu.VMEM((2, clusters, all_users), f32),
            pltpu.VMEM((clusters, user_slots), f32),
            pltpu.VMEM((clusters, user_slots), f32),
            pltpu.VMEM((blocks, block_camps), f32),
            pltpu.VMEM((blocks, block_camps), f32),
            pltpu.VMEM((2 * n, blocks), bf),
            pltpu.VMEM((blocks, 2 * n), bf),
            pltpu.VMEM((blocks, block_camps), f32),
            pltpu.VMEM((blocks, block_camps), f32),
            dma((6,)), dma((2,)), dma, dma, dma, dma, dma, dma, dma, dma, dma, dma,
            dma((5,)), dma((5,)), dma((6,)), dma((6,)), dma, dma,
        ],
        compiler_params=pltpu.CompilerParams(
            collective_id=0, has_side_effects=True, vmem_limit_bytes=56 << 20
        ),
        name="allocate",
    )(
        elig_owner.T, elig_local.T, cluster_size.reshape(1, clusters),
        camp_count.reshape(1, blocks), dual_init, spend_limit, camp_emb, user_emb,
    )


def solution(mesh):
    return jax.shard_map(
        body,
        mesh=mesh,
        in_specs=(
            P("shard", "rep", None),
            P("shard", None),
            P("shard", None),
            P("shard"),
            P("shard", None, None),
            P("shard"),
            P("shard", None),
            P("shard", None),
        ),
        out_specs=(P("shard", "rep"), P("shard", None)),
        check_vma=False,
    )
```

```python
import functools
import math

import jax
import jax.numpy as jnp
from jax import lax
from jax.experimental import pallas as pl
from jax.experimental.pallas import tpu as pltpu
from jax.sharding import PartitionSpec as P

epsilon = 1e-06
temper = 0.25
sharpness = 16.0
mix = 37
MESH = pl.DeviceIdType.MESH


def kernel(
    radix,
    owner_hbm,
    local_hbm,
    size_hbm,
    count_hbm,
    init_hbm,
    limit_hbm,
    camp_hbm,
    user_hbm,
    user_out_hbm,
    dual_out_hbm,
    owner_ref,
    local_ref,
    size_ref,
    count_ref,
    dual_init,
    limits,
    user_out,
    dual_out,
    camps,
    users,
    user_scale,
    sendbuf,
    recvbuf,
    kmat,
    rows_pad,
    wanted,
    slots,
    slots_smem,
    ids_in,
    ids_smem,
    to_slots,
    to_items,
    row_send,
    row_recv,
    den_send,
    den_recv,
    last_send,
    last_recv,
    dual_send,
    dual_recv,
    hit,
    hit_t,
    lam,
    vdup,
    small_sem,
    out_sem,
    camp_sem,
    user_sem,
    smem_sem,
    slot_sem,
    user_ssem,
    user_rsem,
    ids_ssem,
    ids_rsem,
    bulk_ssem,
    bulk_rsem,
    row_ssem,
    row_rsem,
    den_ssem,
    den_rsem,
    dual_ssem,
    dual_rsem,
):
    me = lax.axis_index("shard")
    rep = lax.axis_index("rep")
    n = wanted.shape[0]
    clusters, half_users, width = user_hbm.shape
    all_users = 2 * half_users
    half = camps.shape[1]
    lanes = 2 * half
    blocks = camps.shape[0]

    places = (radix * radix, radix, 1)
    digits = [(me // p) % radix for p in places]
    moved = {
        sign: [
            [((digit + sign * j + radix) % radix) * p for j in range(radix)]
            for digit, p in zip(digits, places)
        ]
        for sign in (1, -1)
    }

    def partner(d, sign):
        return sum(moved[sign][i][(d // p) % radix] for i, p in enumerate(places))

    def hops(d):
        steps = [(d // p) % radix for p in places]
        return sum(min(t, radix - t) for t in steps)

    order = [(i * mix) % n for i in range(1, n)]

    def hops(d):
        steps = [(d // p) % radix for p in places]
        return sum(min(t, radix - t) for t in steps)

    bulk_order = sorted(order, key=lambda d: hops(d) <= 1)
    order = sorted(order, key=lambda d: -hops(d))

    barrier = pltpu.get_barrier_semaphore()
    for d in order:
        pl.semaphore_signal(
            barrier, inc=1, device_id=(partner(d, 1), rep), device_id_type=MESH
        )
    pl.semaphore_signal(barrier, inc=1, device_id=(me, 1 - rep), device_id_type=MESH)

    def fetch(src, dst, i):
        copy = pltpu.make_async_copy(src, dst, small_sem.at[i])
        copy.start()
        return copy

    get_owner = fetch(owner_hbm, owner_ref, 0)
    get_local = fetch(local_hbm, local_ref, 1)
    get_rest = [
        fetch(size_hbm, size_ref, 2), fetch(count_hbm, count_ref, 3),
        fetch(init_hbm, dual_init, 4), fetch(limit_hbm, limits, 5),
    ]
    my_rows = pl.ds(pl.multiple_of(rep * half, half), half)
    my_users = pl.ds(pl.multiple_of(rep * half_users, half_users), half_users)
    load_camps = pltpu.make_async_copy(camp_hbm.at[:, my_rows, :], camps, camp_sem)
    load_camps.start()
    load_users = pltpu.make_async_copy(user_hbm, users.at[:, my_users, :], user_sem)
    load_users.start()

    def remote(src, dst, ssem, rsem, target):
        return pltpu.make_async_remote_copy(
            src_ref=src, dst_ref=dst, send_sem=ssem, recv_sem=rsem,
            device_id=target, device_id_type=MESH,
        )

    def scatter(src, dst, ssem, rsem, sign):
        for d in order:
            remote(src.at[d], dst.at[d], ssem, rsem, (partner(d, sign), rep)).start()

    def all_of(src, dst, ssem, rsem):
        rest = pl.ds(1, n - 1)
        return remote(src.at[rest], dst.at[rest], ssem, rsem, (me, 1 - rep))

    fan, _ = owner_ref.shape
    i32, f32, bf16 = jnp.int32, jnp.float32, jnp.bfloat16
    lane = lax.broadcasted_iota(i32, (1, lanes), 1)
    left = lane < half
    evens, odds = list(range(0, fan, 2)), list(range(1, fan, 2))
    columns = evens + odds + odds + evens

    def column_row(ref):
        rows_pad[...] = jnp.zeros_like(rows_pad)
        rows_pad[0:fan, 0:clusters] = ref[...]
        row = rows_pad[...]
        out = jnp.zeros((1, lanes), i32)
        for at, e in enumerate(columns):
            piece = row[e:e + 1]
            out = out + (pltpu.roll(piece, at * clusters, 1) if at else piece)
        return out

    get_owner.wait()
    get_local.wait()
    owner = column_row(owner_ref)
    local = column_row(local_ref)
    dist = jnp.zeros_like(owner)
    shift = radix.bit_length() - 1
    for i, p in enumerate(places):
        digit = lax.shift_right_logical(owner, i32(p.bit_length() - 1)) & (radix - 1)
        dist = dist + ((digits[i] - digit + radix) & (radix - 1)) * p
    mask = dist == lax.broadcasted_iota(i32, (n, lanes), 0)
    from_col = lax.broadcasted_iota(i32, (lanes, lanes), 0)
    to_col = lax.broadcasted_iota(i32, (lanes, lanes), 1)
    cluster_of = clusters - 1
    ahead = (from_col < half) & ((from_col & cluster_of) < (to_col & cluster_of))
    prefix = jnp.dot(
        mask.astype(f32).astype(bf16), ahead.astype(f32).astype(bf16),
        preferred_element_type=f32)
    rank = (lane >= half).astype(i32)
    chosen = mask & (prefix == rank.astype(f32))
    to_slots[...] = chosen.astype(f32).astype(bf16)
    to_items[...] = chosen.astype(f32).T.astype(bf16)
    first = jnp.sum(jnp.where(chosen & left, local, 0), axis=1, keepdims=True)
    second = jnp.sum(jnp.where(chosen & ~left, local, 0), axis=1, keepdims=True)
    wanted[:, 0, :] = jnp.where(lane == 0, first, second)
    slot = lax.broadcasted_iota(i32, (n, lanes), 0) * 2 + rank
    slots[...] = jnp.sum(jnp.where(chosen, slot, 0), axis=0, keepdims=True)
    slots_to_smem = pltpu.make_async_copy(slots, slots_smem, slot_sem)
    slots_to_smem.start()

    pl.semaphore_wait(barrier, n)

    scatter(wanted, ids_in, ids_ssem, ids_rsem, -1)
    swap_users = remote(
        user_hbm, users.at[:, my_users, :], user_ssem, user_rsem, (me, 1 - rep)
    )
    swap_users.start()
    ids_in[0] = wanted[0]

    def spread(x):
        rolled = pltpu.roll(x, half, 1)
        mine = left == (rep == 0)
        return jnp.where(mine, x, rolled)

    for copy in get_rest:
        copy.wait()
    lam[...] = spread(dual_init[...])
    limit = spread(limits[...])
    diagonal = from_col == to_col

    def column(row):
        return jnp.sum(jnp.where(diagonal[:blocks], row.astype(f32), 0.0), axis=1, keepdims=True)

    counts = column(count_ref[...])
    camp_pos = jnp.where(left, lane, lane - half) + rep * half
    live_camps = camp_pos.astype(f32) < counts

    def weights_of(duals):
        return jnp.where(live_camps, jnp.exp(duals * (-1.0 / temper)), 0.0)

    vdup[...] = weights_of(lam[...])

    all_of(wanted, ids_in, ids_ssem, ids_rsem).wait()
    to_smem = pltpu.make_async_copy(ids_in, ids_smem, smem_sem)
    to_smem.start()
    def pick(table, x):
        upper = x.astype(bf16)
        lower = (x - upper.astype(f32)).astype(bf16)
        out = jnp.dot(
            table, jnp.concatenate([upper, lower], axis=1), preferred_element_type=f32)
        return out[:, :lanes] + out[:, lanes:]

    def send_weights(step):
        picked = pick(hit[...], vdup[...])
        row_send[step, :, 0, :] = jnp.where(left, picked[:n], picked[n:])
        scatter(row_send.at[step], row_recv.at[step], row_ssem.at[step], row_rsem.at[step], 1)
        row_recv[step, 0] = row_send[step, 0]

    def wait_rows(step):
        all_of(
            row_send.at[step], row_recv.at[step], row_ssem.at[step], row_rsem.at[step]
        ).wait()
        return row_recv[step, :, 0, :]

    to_smem.wait()
    load_camps.wait()

    def clamp(i, size):
        return jnp.minimum(jnp.maximum(i, 0), size - 1)

    for d in bulk_order:
        for j in range(2):
            sendbuf[2 * d + j] = camps[clamp(ids_smem[d, 0, j], blocks)]
        pair = pl.ds(2 * d, 2)
        remote(
            sendbuf.at[pair], recvbuf.at[pair], bulk_ssem, bulk_rsem, (partner(d, 1), rep)
        ).start()

    for j in range(2):
        recvbuf[j] = camps[clamp(ids_smem[0, 0, j], blocks)]

    ids = ids_in[:, 0, :]
    block_ids = lax.broadcasted_iota(jnp.int32, (n, blocks), 1)
    hits = jnp.concatenate(
        [(jnp.broadcast_to(ids[:, j:j + 1], (n, blocks)) == block_ids).astype(f32)
         for j in range(2)], axis=0)
    hit[...] = hits.astype(bf16)
    hit_t[...] = hits.T.astype(bf16)
    send_weights(0)
    load_users.wait()
    swap_users.wait()

    chunk = 256 if all_users % 256 == 0 else all_users
    chunks = all_users // chunk

    @pl.loop(0, clusters * chunks)
    def _(i):
        k = i // chunks
        at = pl.ds(pl.multiple_of((i % chunks) * chunk, chunk), chunk)
        x = users[k, at, :].astype(jnp.float32)
        mean = jnp.sum(x * x, axis=1, keepdims=True) * (1.0 / width)
        user_scale[k, at, :] = jnp.broadcast_to(lax.rsqrt(mean + epsilon), (chunk, 128))

    rest = pl.ds(2, 2 * n - 2)
    remote(sendbuf.at[rest], recvbuf.at[rest], bulk_ssem, bulk_rsem, (me, 1 - rep)).wait()

    factor = sharpness / width / temper * math.log2(math.e)
    cols = fan * half

    slots_to_smem.wait()
    first_at = [columns.index(e) * clusters for e in range(fan)]
    second_at = [(columns.index(e, fan)) * clusters for e in range(fan)]

    @pl.loop(0, clusters, unroll=8)
    def _(k):
        emb = jnp.concatenate(
            [recvbuf[clamp(
                slots_smem[0, first_at[e] + k] + slots_smem[0, second_at[e] + k], 2 * n)]
             for e in range(fan)], axis=0)
        wide = emb.astype(jnp.float32)
        square = wide * wide
        upper = square.astype(jnp.bfloat16)
        lower = (square - upper.astype(jnp.float32)).astype(jnp.bfloat16)
        ones = jnp.ones((16, width), jnp.bfloat16)
        dims = (((1,), (1,)), ((), ()))
        total = lax.dot_general(ones, upper, dims, preferred_element_type=jnp.float32)
        total = total + lax.dot_general(ones, lower, dims, preferred_element_type=jnp.float32)
        camp_scale = lax.rsqrt(total[0:1] * (1.0 / width) + epsilon) * factor
        for c in range(chunks):
            at = pl.ds(c * chunk, chunk)
            raw = lax.dot_general(users[k, at, :], emb, dims, preferred_element_type=jnp.float32)
            scale = user_scale[k, at, :]
            wide_scale = jnp.concatenate([scale] * (cols // 128), axis=1)
            kmat[k, at, :] = jnp.exp2(raw * wide_scale * camp_scale).astype(jnp.bfloat16)

    def split(x):
        upper = x.astype(bf16).astype(f32)
        return jnp.concatenate([upper, x - upper], axis=0).astype(bf16)

    part = fan * clusters // 2
    group = clusters // 2
    row_id = lax.broadcasted_iota(i32, (group, 1), 0)

    sizes = jnp.sum(
        jnp.where(diagonal[:clusters, :clusters], size_ref[...].astype(f32), 0.0),
        axis=1, keepdims=True).astype(i32)
    live_users = lax.broadcasted_iota(i32, (clusters, all_users), 1) < sizes

    def item_weights(rows):
        picked = pick(to_items[...], rows)
        a, b, c, d = [picked[p * part:(p + 1) * part] for p in range(4)]
        table = jnp.where(left, a + pltpu.roll(d, half, 1), c + pltpu.roll(b, half, 1))
        return jnp.concatenate(
            [table[p * clusters:(p + 1) * clusters] for p in range(fan // 2)], axis=1)

    def partial_sums(v, h):
        at = h * group
        lhs = split(v[at:at + group])

        def add(k, acc):
            out = lax.dot_general(
                lhs, kmat[k], (((1,), (1,)), ((), ())), preferred_element_type=f32)
            return acc + jnp.where(row_id == k - at, out[:group] + out[group:], 0.0)

        zero = jnp.zeros((group, all_users), f32)
        return lax.fori_loop(at, at + group, add, zero, unroll=8)

    def sweep(step, rows):
        v = item_weights(rows)
        own, swaps, sums = [], [], []
        for h in range(2):
            own.append(partial_sums(v, h))
            at = pl.ds(h * group, group)
            den_send[step, at] = own[h]
            swaps.append(remote(
                den_send.at[step, at], den_recv.at[step, at],
                den_ssem.at[2 * step + h], den_rsem.at[2 * step + h], (me, 1 - rep)))
            swaps[h].start()
        for h in range(2):
            at = h * group
            swaps[h].wait()
            den = 1.0 + (own[h] + den_recv[step, at:at + group])
            q = split(jnp.where(live_users[at:at + group], 1.0 / den, 0.0))

            def add(k, acc, q=q, at=at):
                out = jnp.dot(q, kmat[k], preferred_element_type=f32)
                return acc + jnp.where(row_id == k - at, out[:group] + out[group:], 0.0)

            sums.append(lax.fori_loop(
                at, at + group, add, jnp.zeros((group, cols), f32), unroll=8))
        sums = jnp.concatenate(sums, axis=0)
        table = jnp.concatenate(
            [sums[:, p * lanes:(p + 1) * lanes] for p in range(fan // 2)], axis=0)
        rolled = pltpu.roll(table, half, 1)
        zero = jnp.zeros_like(table)
        stack = jnp.concatenate(
            [jnp.where(left, table, zero), jnp.where(left, rolled, zero),
             jnp.where(left, zero, table), jnp.where(left, zero, rolled)], axis=0)
        out = pick(to_slots[...], stack)
        at = 2 * step + 1
        row_send[at, :, 0, :] = out
        scatter(row_send.at[at], row_recv.at[at], row_ssem.at[at], row_rsem.at[at], -1)
        row_recv[at, 0] = row_send[at, 0]
        got = wait_rows(at)
        turned = pltpu.roll(got, half, 1)
        both = jnp.concatenate(
            [jnp.where(left, got, turned), jnp.where(left, turned, got)], axis=0)
        spend = vdup[...] * pick(hit_t[...], both)
        duals = jnp.maximum(
            0.0, lam[...] + temper * jnp.log((spend + limit) / (2.0 * limit)))
        lam[...] = duals
        vdup[...] = weights_of(duals)
        send_weights(at + 1)

    sweep(0, wait_rows(0))
    sweep(1, wait_rows(2))
    dual_send[...] = lam[...]
    swap_duals = remote(dual_send, dual_recv, dual_ssem, dual_rsem, (me, 1 - rep))
    swap_duals.start()
    v = item_weights(wait_rows(4))
    mine, swaps = [], []
    for h in range(2):
        own = partial_sums(v, h)
        low, high = own[:, :half_users], own[:, half_users:]
        mine.append(jnp.where(rep == 0, low, high))
        at = pl.ds(h * group, group)
        last_send[at] = jnp.where(rep == 0, high, low)
        swaps.append(remote(
            last_send.at[at], last_recv.at[at], den_ssem.at[4 + h], den_rsem.at[4 + h],
            (me, 1 - rep)))
        swaps[h].start()
    swap_duals.wait()
    dual_out[...] = jnp.where(left == (rep == 0), dual_send[...], dual_recv[...])
    put_duals = pltpu.make_async_copy(dual_out, dual_out_hbm, out_sem.at[0])
    put_duals.start()
    user_pos = lax.broadcasted_iota(i32, (clusters, half_users), 1) + rep * half_users
    for h in range(2):
        at = h * group
        swaps[h].wait()
        den = 1.0 + (mine[h] + last_recv[at:at + group])
        user_out[at:at + group] = jnp.where(
            user_pos[at:at + group] < sizes[at:at + group], temper * jnp.log(den), 0.0)
    put_users = pltpu.make_async_copy(user_out, user_out_hbm, out_sem.at[1])
    put_users.start()
    put_duals.wait()
    put_users.wait()


def body(
    user_emb, elig_owner, elig_local, cluster_size, camp_emb, camp_count, dual_init, spend_limit
):
    n = lax.axis_size("shard")
    radix = round(n ** (1 / 3))
    clusters, user_slots, width = user_emb.shape
    blocks, block_camps, _ = camp_emb.shape
    fan = elig_owner.shape[1]
    half = block_camps // 2
    hbm = pl.BlockSpec(memory_space=pl.ANY)
    bf, f32, i32 = jnp.bfloat16, jnp.float32, jnp.int32
    dma = pltpu.SemaphoreType.DMA
    all_users = 2 * user_slots
    return pl.pallas_call(
        functools.partial(kernel, radix),
        out_shape=(
            jax.ShapeDtypeStruct((clusters, user_slots), f32),
            jax.ShapeDtypeStruct((blocks, block_camps), f32),
        ),
        in_specs=[hbm] * 8,
        out_specs=(hbm, hbm),
        scratch_shapes=[
            pltpu.VMEM((fan, clusters), i32),
            pltpu.VMEM((fan, clusters), i32),
            pltpu.VMEM((1, clusters), i32),
            pltpu.VMEM((1, blocks), i32),
            pltpu.VMEM((blocks, block_camps), f32),
            pltpu.VMEM((blocks, block_camps), f32),
            pltpu.VMEM((clusters, user_slots), f32),
            pltpu.VMEM((blocks, block_camps), f32),
            pltpu.VMEM((blocks, half, width), bf),
            pltpu.VMEM((clusters, all_users, width), bf),
            pltpu.VMEM((clusters, all_users, 128), f32),
            pltpu.VMEM((2 * n, half, width), bf),
            pltpu.VMEM((2 * n, half, width), bf),
            pltpu.VMEM((clusters, all_users, fan * half), bf),
            pltpu.VMEM((8, 128), i32),
            pltpu.VMEM((n, 1, 128), i32),
            pltpu.VMEM((1, 128), i32),
            pltpu.SMEM((1, 128), i32),
            pltpu.VMEM((n, 1, 128), i32),
            pltpu.SMEM((n, 1, 128), i32),
            pltpu.VMEM((n, 128), bf),
            pltpu.VMEM((128, n), bf),
            pltpu.VMEM((5, n, 1, block_camps), f32),
            pltpu.VMEM((5, n, 1, block_camps), f32),
            pltpu.VMEM((2, clusters, all_users), f32),
            pltpu.VMEM((2, clusters, all_users), f32),
            pltpu.VMEM((clusters, user_slots), f32),
            pltpu.VMEM((clusters, user_slots), f32),
            pltpu.VMEM((blocks, block_camps), f32),
            pltpu.VMEM((blocks, block_camps), f32),
            pltpu.VMEM((2 * n, blocks), bf),
            pltpu.VMEM((blocks, 2 * n), bf),
            pltpu.VMEM((blocks, block_camps), f32),
            pltpu.VMEM((blocks, block_camps), f32),
            dma((6,)), dma((2,)), dma, dma, dma, dma, dma, dma, dma, dma, dma, dma,
            dma((5,)), dma((5,)), dma((6,)), dma((6,)), dma, dma,
        ],
        compiler_params=pltpu.CompilerParams(
            collective_id=0, has_side_effects=True, vmem_limit_bytes=56 << 20
        ),
        name="allocate",
    )(
        elig_owner.T, elig_local.T, cluster_size.reshape(1, clusters),
        camp_count.reshape(1, blocks), dual_init, spend_limit, camp_emb, user_emb,
    )


def solution(mesh):
    return jax.shard_map(
        body,
        mesh=mesh,
        in_specs=(
            P("shard", "rep", None),
            P("shard", None),
            P("shard", None),
            P("shard"),
            P("shard", None, None),
            P("shard"),
            P("shard", None),
            P("shard", None),
        ),
        out_specs=(P("shard", "rep"), P("shard", None)),
        check_vma=False,
    )
```

```python
import functools
import math

import jax
import jax.numpy as jnp
from jax import lax
from jax.experimental import pallas as pl
from jax.experimental.pallas import tpu as pltpu
from jax.sharding import PartitionSpec as P

epsilon = 1e-06
temper = 0.25
sharpness = 16.0
mix = 37
MESH = pl.DeviceIdType.MESH


def kernel(
    radix,
    owner_hbm,
    local_hbm,
    size_hbm,
    count_hbm,
    init_hbm,
    limit_hbm,
    camp_hbm,
    user_hbm,
    user_out_hbm,
    dual_out_hbm,
    owner_ref,
    local_ref,
    size_ref,
    count_ref,
    dual_init,
    limits,
    user_out,
    dual_out,
    camps,
    users,
    user_scale,
    sendbuf,
    recvbuf,
    kmat,
    rows_pad,
    wanted,
    slots,
    slots_smem,
    ids_in,
    ids_smem,
    to_slots,
    to_items,
    row_send,
    row_recv,
    den_send,
    den_recv,
    last_send,
    last_recv,
    dual_send,
    dual_recv,
    hit,
    hit_t,
    lam,
    vdup,
    small_sem,
    out_sem,
    camp_sem,
    user_sem,
    smem_sem,
    slot_sem,
    user_ssem,
    user_rsem,
    ids_ssem,
    ids_rsem,
    bulk_ssem,
    bulk_rsem,
    row_ssem,
    row_rsem,
    den_ssem,
    den_rsem,
    dual_ssem,
    dual_rsem,
):
    me = lax.axis_index("shard")
    rep = lax.axis_index("rep")
    n = wanted.shape[0]
    clusters, half_users, width = user_hbm.shape
    all_users = 2 * half_users
    half = camps.shape[1]
    lanes = 2 * half
    blocks = camps.shape[0]

    places = (radix * radix, radix, 1)
    digits = [(me // p) % radix for p in places]
    moved = {
        sign: [
            [((digit + sign * j + radix) % radix) * p for j in range(radix)]
            for digit, p in zip(digits, places)
        ]
        for sign in (1, -1)
    }

    def partner(d, sign):
        return sum(moved[sign][i][(d // p) % radix] for i, p in enumerate(places))

    def hops(d):
        steps = [(d // p) % radix for p in places]
        return sum(min(t, radix - t) for t in steps)

    order = [(i * mix) % n for i in range(1, n)]

    def hops(d):
        steps = [(d // p) % radix for p in places]
        return sum(min(t, radix - t) for t in steps)

    bulk_order = sorted(order, key=lambda d: hops(d) <= 1)
    order = sorted(order, key=lambda d: -hops(d))

    barrier = pltpu.get_barrier_semaphore()
    for d in order:
        pl.semaphore_signal(
            barrier, inc=1, device_id=(partner(d, 1), rep), device_id_type=MESH
        )
    pl.semaphore_signal(barrier, inc=1, device_id=(me, 1 - rep), device_id_type=MESH)

    def fetch(src, dst, i):
        copy = pltpu.make_async_copy(src, dst, small_sem.at[i])
        copy.start()
        return copy

    get_owner = fetch(owner_hbm, owner_ref, 0)
    get_local = fetch(local_hbm, local_ref, 1)
    get_rest = [
        fetch(size_hbm, size_ref, 2), fetch(count_hbm, count_ref, 3),
        fetch(init_hbm, dual_init, 4), fetch(limit_hbm, limits, 5),
    ]
    my_rows = pl.ds(pl.multiple_of(rep * half, half), half)
    my_users = pl.ds(pl.multiple_of(rep * half_users, half_users), half_users)
    load_camps = pltpu.make_async_copy(camp_hbm.at[:, my_rows, :], camps, camp_sem)
    load_camps.start()
    load_users = pltpu.make_async_copy(user_hbm, users.at[:, my_users, :], user_sem)
    load_users.start()

    def remote(src, dst, ssem, rsem, target):
        return pltpu.make_async_remote_copy(
            src_ref=src, dst_ref=dst, send_sem=ssem, recv_sem=rsem,
            device_id=target, device_id_type=MESH,
        )

    def scatter(src, dst, ssem, rsem, sign):
        for d in order:
            remote(src.at[d], dst.at[d], ssem, rsem, (partner(d, sign), rep)).start()

    def all_of(src, dst, ssem, rsem):
        rest = pl.ds(1, n - 1)
        return remote(src.at[rest], dst.at[rest], ssem, rsem, (me, 1 - rep))

    fan, _ = owner_ref.shape
    i32, f32, bf16 = jnp.int32, jnp.float32, jnp.bfloat16
    lane = lax.broadcasted_iota(i32, (1, lanes), 1)
    left = lane < half
    evens, odds = list(range(0, fan, 2)), list(range(1, fan, 2))
    columns = evens + odds + odds + evens

    def column_row(ref):
        rows_pad[...] = jnp.zeros_like(rows_pad)
        rows_pad[0:fan, 0:clusters] = ref[...]
        row = rows_pad[...]
        out = jnp.zeros((1, lanes), i32)
        for at, e in enumerate(columns):
            piece = row[e:e + 1]
            out = out + (pltpu.roll(piece, at * clusters, 1) if at else piece)
        return out

    get_owner.wait()
    get_local.wait()
    owner = column_row(owner_ref)
    local = column_row(local_ref)
    dist = jnp.zeros_like(owner)
    shift = radix.bit_length() - 1
    for i, p in enumerate(places):
        digit = lax.shift_right_logical(owner, i32(p.bit_length() - 1)) & (radix - 1)
        dist = dist + ((digits[i] - digit + radix) & (radix - 1)) * p
    mask = dist == lax.broadcasted_iota(i32, (n, lanes), 0)
    from_col = lax.broadcasted_iota(i32, (lanes, lanes), 0)
    to_col = lax.broadcasted_iota(i32, (lanes, lanes), 1)
    cluster_of = clusters - 1
    ahead = (from_col < half) & ((from_col & cluster_of) < (to_col & cluster_of))
    prefix = jnp.dot(
        mask.astype(f32).astype(bf16), ahead.astype(f32).astype(bf16),
        preferred_element_type=f32)
    rank = (lane >= half).astype(i32)
    chosen = mask & (prefix == rank.astype(f32))
    to_slots[...] = chosen.astype(f32).astype(bf16)
    to_items[...] = chosen.astype(f32).T.astype(bf16)
    first = jnp.sum(jnp.where(chosen & left, local, 0), axis=1, keepdims=True)
    second = jnp.sum(jnp.where(chosen & ~left, local, 0), axis=1, keepdims=True)
    wanted[:, 0, :] = jnp.where(lane == 0, first, second)
    slot = lax.broadcasted_iota(i32, (n, lanes), 0) * 2 + rank
    slots[...] = jnp.sum(jnp.where(chosen, slot, 0), axis=0, keepdims=True)
    slots_to_smem = pltpu.make_async_copy(slots, slots_smem, slot_sem)
    slots_to_smem.start()

    pl.semaphore_wait(barrier, n)

    scatter(wanted, ids_in, ids_ssem, ids_rsem, -1)
    swap_users = remote(
        user_hbm, users.at[:, my_users, :], user_ssem, user_rsem, (me, 1 - rep)
    )
    swap_users.start()
    ids_in[0] = wanted[0]

    def spread(x):
        rolled = pltpu.roll(x, half, 1)
        mine = left == (rep == 0)
        return jnp.where(mine, x, rolled)

    for copy in get_rest:
        copy.wait()
    lam[...] = spread(dual_init[...])
    limit = spread(limits[...])
    diagonal = from_col == to_col

    def column(row):
        return jnp.sum(jnp.where(diagonal[:blocks], row.astype(f32), 0.0), axis=1, keepdims=True)

    counts = column(count_ref[...])
    camp_pos = jnp.where(left, lane, lane - half) + rep * half
    live_camps = camp_pos.astype(f32) < counts

    def weights_of(duals):
        return jnp.where(live_camps, jnp.exp(duals * (-1.0 / temper)), 0.0)

    vdup[...] = weights_of(lam[...])

    all_of(wanted, ids_in, ids_ssem, ids_rsem).wait()
    to_smem = pltpu.make_async_copy(ids_in, ids_smem, smem_sem)
    to_smem.start()
    def pick(table, x):
        upper = x.astype(bf16)
        lower = (x - upper.astype(f32)).astype(bf16)
        out = jnp.dot(
            table, jnp.concatenate([upper, lower], axis=1), preferred_element_type=f32)
        return out[:, :lanes] + out[:, lanes:]

    def send_weights(step):
        picked = pick(hit[...], vdup[...])
        row_send[step, :, 0, :] = jnp.where(left, picked[:n], picked[n:])
        scatter(row_send.at[step], row_recv.at[step], row_ssem.at[step], row_rsem.at[step], 1)
        row_recv[step, 0] = row_send[step, 0]

    def wait_rows(step):
        all_of(
            row_send.at[step], row_recv.at[step], row_ssem.at[step], row_rsem.at[step]
        ).wait()
        return row_recv[step, :, 0, :]

    to_smem.wait()
    load_camps.wait()

    def clamp(i, size):
        return jnp.minimum(jnp.maximum(i, 0), size - 1)

    for d in bulk_order:
        for j in range(2):
            sendbuf[2 * d + j] = camps[clamp(ids_smem[d, 0, j], blocks)]
            remote(
                sendbuf.at[2 * d + j], recvbuf.at[2 * d + j], bulk_ssem, bulk_rsem,
                (partner(d, 1), rep),
            ).start()

    for j in range(2):
        recvbuf[j] = camps[clamp(ids_smem[0, 0, j], blocks)]

    ids = ids_in[:, 0, :]
    block_ids = lax.broadcasted_iota(jnp.int32, (n, blocks), 1)
    hits = jnp.concatenate(
        [(jnp.broadcast_to(ids[:, j:j + 1], (n, blocks)) == block_ids).astype(f32)
         for j in range(2)], axis=0)
    hit[...] = hits.astype(bf16)
    hit_t[...] = hits.T.astype(bf16)
    send_weights(0)
    load_users.wait()
    swap_users.wait()

    chunk = 256 if all_users % 256 == 0 else all_users
    chunks = all_users // chunk

    @pl.loop(0, clusters * chunks)
    def _(i):
        k = i // chunks
        at = pl.ds(pl.multiple_of((i % chunks) * chunk, chunk), chunk)
        x = users[k, at, :].astype(jnp.float32)
        mean = jnp.sum(x * x, axis=1, keepdims=True) * (1.0 / width)
        user_scale[k, at, :] = jnp.broadcast_to(lax.rsqrt(mean + epsilon), (chunk, 128))

    rest = pl.ds(2, 2 * n - 2)
    remote(sendbuf.at[rest], recvbuf.at[rest], bulk_ssem, bulk_rsem, (me, 1 - rep)).wait()

    factor = sharpness / width / temper * math.log2(math.e)
    cols = fan * half

    slots_to_smem.wait()
    first_at = [columns.index(e) * clusters for e in range(fan)]
    second_at = [(columns.index(e, fan)) * clusters for e in range(fan)]

    @pl.loop(0, clusters, unroll=8)
    def _(k):
        emb = jnp.concatenate(
            [recvbuf[clamp(
                slots_smem[0, first_at[e] + k] + slots_smem[0, second_at[e] + k], 2 * n)]
             for e in range(fan)], axis=0)
        wide = emb.astype(jnp.float32)
        square = wide * wide
        upper = square.astype(jnp.bfloat16)
        lower = (square - upper.astype(jnp.float32)).astype(jnp.bfloat16)
        ones = jnp.ones((16, width), jnp.bfloat16)
        dims = (((1,), (1,)), ((), ()))
        total = lax.dot_general(ones, upper, dims, preferred_element_type=jnp.float32)
        total = total + lax.dot_general(ones, lower, dims, preferred_element_type=jnp.float32)
        camp_scale = lax.rsqrt(total[0:1] * (1.0 / width) + epsilon) * factor
        for c in range(chunks):
            at = pl.ds(c * chunk, chunk)
            raw = lax.dot_general(users[k, at, :], emb, dims, preferred_element_type=jnp.float32)
            scale = user_scale[k, at, :]
            wide_scale = jnp.concatenate([scale] * (cols // 128), axis=1)
            kmat[k, at, :] = jnp.exp2(raw * wide_scale * camp_scale).astype(jnp.bfloat16)

    def split(x):
        upper = x.astype(bf16).astype(f32)
        return jnp.concatenate([upper, x - upper], axis=0).astype(bf16)

    part = fan * clusters // 2
    group = clusters // 2
    row_id = lax.broadcasted_iota(i32, (group, 1), 0)

    sizes = jnp.sum(
        jnp.where(diagonal[:clusters, :clusters], size_ref[...].astype(f32), 0.0),
        axis=1, keepdims=True).astype(i32)
    live_users = lax.broadcasted_iota(i32, (clusters, all_users), 1) < sizes

    def item_weights(rows):
        picked = pick(to_items[...], rows)
        a, b, c, d = [picked[p * part:(p + 1) * part] for p in range(4)]
        table = jnp.where(left, a + pltpu.roll(d, half, 1), c + pltpu.roll(b, half, 1))
        return jnp.concatenate(
            [table[p * clusters:(p + 1) * clusters] for p in range(fan // 2)], axis=1)

    def partial_sums(v, h):
        at = h * group
        lhs = split(v[at:at + group])

        def add(k, acc):
            out = lax.dot_general(
                lhs, kmat[k], (((1,), (1,)), ((), ())), preferred_element_type=f32)
            return acc + jnp.where(row_id == k - at, out[:group] + out[group:], 0.0)

        zero = jnp.zeros((group, all_users), f32)
        return lax.fori_loop(at, at + group, add, zero, unroll=8)

    def sweep(step, rows):
        v = item_weights(rows)
        own, swaps, sums = [], [], []
        for h in range(2):
            own.append(partial_sums(v, h))
            at = pl.ds(h * group, group)
            den_send[step, at] = own[h]
            swaps.append(remote(
                den_send.at[step, at], den_recv.at[step, at],
                den_ssem.at[2 * step + h], den_rsem.at[2 * step + h], (me, 1 - rep)))
            swaps[h].start()
        for h in range(2):
            at = h * group
            swaps[h].wait()
            den = 1.0 + (own[h] + den_recv[step, at:at + group])
            q = split(jnp.where(live_users[at:at + group], 1.0 / den, 0.0))

            def add(k, acc, q=q, at=at):
                out = jnp.dot(q, kmat[k], preferred_element_type=f32)
                return acc + jnp.where(row_id == k - at, out[:group] + out[group:], 0.0)

            sums.append(lax.fori_loop(
                at, at + group, add, jnp.zeros((group, cols), f32), unroll=8))
        sums = jnp.concatenate(sums, axis=0)
        table = jnp.concatenate(
            [sums[:, p * lanes:(p + 1) * lanes] for p in range(fan // 2)], axis=0)
        rolled = pltpu.roll(table, half, 1)
        zero = jnp.zeros_like(table)
        stack = jnp.concatenate(
            [jnp.where(left, table, zero), jnp.where(left, rolled, zero),
             jnp.where(left, zero, table), jnp.where(left, zero, rolled)], axis=0)
        out = pick(to_slots[...], stack)
        at = 2 * step + 1
        row_send[at, :, 0, :] = out
        scatter(row_send.at[at], row_recv.at[at], row_ssem.at[at], row_rsem.at[at], -1)
        row_recv[at, 0] = row_send[at, 0]
        got = wait_rows(at)
        turned = pltpu.roll(got, half, 1)
        both = jnp.concatenate(
            [jnp.where(left, got, turned), jnp.where(left, turned, got)], axis=0)
        spend = vdup[...] * pick(hit_t[...], both)
        duals = jnp.maximum(
            0.0, lam[...] + temper * jnp.log((spend + limit) / (2.0 * limit)))
        lam[...] = duals
        vdup[...] = weights_of(duals)
        send_weights(at + 1)

    sweep(0, wait_rows(0))
    sweep(1, wait_rows(2))
    dual_send[...] = lam[...]
    swap_duals = remote(dual_send, dual_recv, dual_ssem, dual_rsem, (me, 1 - rep))
    swap_duals.start()
    v = item_weights(wait_rows(4))
    mine, swaps = [], []
    for h in range(2):
        own = partial_sums(v, h)
        low, high = own[:, :half_users], own[:, half_users:]
        mine.append(jnp.where(rep == 0, low, high))
        at = pl.ds(h * group, group)
        last_send[at] = jnp.where(rep == 0, high, low)
        swaps.append(remote(
            last_send.at[at], last_recv.at[at], den_ssem.at[4 + h], den_rsem.at[4 + h],
            (me, 1 - rep)))
        swaps[h].start()
    swap_duals.wait()
    dual_out[...] = jnp.where(left == (rep == 0), dual_send[...], dual_recv[...])
    put_duals = pltpu.make_async_copy(dual_out, dual_out_hbm, out_sem.at[0])
    put_duals.start()
    user_pos = lax.broadcasted_iota(i32, (clusters, half_users), 1) + rep * half_users
    for h in range(2):
        at = h * group
        swaps[h].wait()
        den = 1.0 + (mine[h] + last_recv[at:at + group])
        user_out[at:at + group] = jnp.where(
            user_pos[at:at + group] < sizes[at:at + group], temper * jnp.log(den), 0.0)
    put_users = pltpu.make_async_copy(user_out, user_out_hbm, out_sem.at[1])
    put_users.start()
    put_duals.wait()
    put_users.wait()


def body(
    user_emb, elig_owner, elig_local, cluster_size, camp_emb, camp_count, dual_init, spend_limit
):
    n = lax.axis_size("shard")
    radix = round(n ** (1 / 3))
    clusters, user_slots, width = user_emb.shape
    blocks, block_camps, _ = camp_emb.shape
    fan = elig_owner.shape[1]
    half = block_camps // 2
    hbm = pl.BlockSpec(memory_space=pl.ANY)
    bf, f32, i32 = jnp.bfloat16, jnp.float32, jnp.int32
    dma = pltpu.SemaphoreType.DMA
    all_users = 2 * user_slots
    return pl.pallas_call(
        functools.partial(kernel, radix),
        out_shape=(
            jax.ShapeDtypeStruct((clusters, user_slots), f32),
            jax.ShapeDtypeStruct((blocks, block_camps), f32),
        ),
        in_specs=[hbm] * 8,
        out_specs=(hbm, hbm),
        scratch_shapes=[
            pltpu.VMEM((fan, clusters), i32),
            pltpu.VMEM((fan, clusters), i32),
            pltpu.VMEM((1, clusters), i32),
            pltpu.VMEM((1, blocks), i32),
            pltpu.VMEM((blocks, block_camps), f32),
            pltpu.VMEM((blocks, block_camps), f32),
            pltpu.VMEM((clusters, user_slots), f32),
            pltpu.VMEM((blocks, block_camps), f32),
            pltpu.VMEM((blocks, half, width), bf),
            pltpu.VMEM((clusters, all_users, width), bf),
            pltpu.VMEM((clusters, all_users, 128), f32),
            pltpu.VMEM((2 * n, half, width), bf),
            pltpu.VMEM((2 * n, half, width), bf),
            pltpu.VMEM((clusters, all_users, fan * half), bf),
            pltpu.VMEM((8, 128), i32),
            pltpu.VMEM((n, 1, 128), i32),
            pltpu.VMEM((1, 128), i32),
            pltpu.SMEM((1, 128), i32),
            pltpu.VMEM((n, 1, 128), i32),
            pltpu.SMEM((n, 1, 128), i32),
            pltpu.VMEM((n, 128), bf),
            pltpu.VMEM((128, n), bf),
            pltpu.VMEM((5, n, 1, block_camps), f32),
            pltpu.VMEM((5, n, 1, block_camps), f32),
            pltpu.VMEM((2, clusters, all_users), f32),
            pltpu.VMEM((2, clusters, all_users), f32),
            pltpu.VMEM((clusters, user_slots), f32),
            pltpu.VMEM((clusters, user_slots), f32),
            pltpu.VMEM((blocks, block_camps), f32),
            pltpu.VMEM((blocks, block_camps), f32),
            pltpu.VMEM((2 * n, blocks), bf),
            pltpu.VMEM((blocks, 2 * n), bf),
            pltpu.VMEM((blocks, block_camps), f32),
            pltpu.VMEM((blocks, block_camps), f32),
            dma((6,)), dma((2,)), dma, dma, dma, dma, dma, dma, dma, dma, dma, dma,
            dma((5,)), dma((5,)), dma((6,)), dma((6,)), dma, dma,
        ],
        compiler_params=pltpu.CompilerParams(
            collective_id=0, has_side_effects=True, vmem_limit_bytes=56 << 20
        ),
        name="allocate",
    )(
        elig_owner.T, elig_local.T, cluster_size.reshape(1, clusters),
        camp_count.reshape(1, blocks), dual_init, spend_limit, camp_emb, user_emb,
    )


def solution(mesh):
    return jax.shard_map(
        body,
        mesh=mesh,
        in_specs=(
            P("shard", "rep", None),
            P("shard", None),
            P("shard", None),
            P("shard"),
            P("shard", None, None),
            P("shard"),
            P("shard", None),
            P("shard", None),
        ),
        out_specs=(P("shard", "rep"), P("shard", None)),
        check_vma=False,
    )
```
